32 devices in a mesh: dp: 4 (over y, core), fsdp: 8 (over z, x).
Axes of the slice: x: 2, y: 2, z: 4, core: 2. Of those that a mesh axis runs over, the one named last changes fastest.
Arguments:
- words: bfloat16 [128, 20, 768], P(('dp', 'fsdp')), may hold values from -6 to 6
- regions: bfloat16 [128, 36, 768], P(('dp', 'fsdp')), may hold values from -6 to 6
- word_count: int32 [128], P(('dp', 'fsdp')), may hold values from 5 to 20, as said below
- region_count: int32 [128], P(('dp', 'fsdp')), may hold values from 10 to 36, as said below
- attn_qkv: bfloat16 [3, 3, 768, 768], P(None, None, 'fsdp'), may hold values from -0.21875 to 0.21875
- attn_out: bfloat16 [3, 768, 768], P(None, 'fsdp'), may hold values from -0.625 to 0.625
- attn_bias: bfloat16 [3, 3, 768], P(None, None, 'fsdp'), may hold values from -3 to 3
- ffn_in: bfloat16 [2, 768, 3072], P(None, 'fsdp'), may hold values from -0.21875 to 0.21875
- ffn_in_bias: bfloat16 [2, 3072], P(None, 'fsdp'), may hold values from -3 to 3
- ffn_out: bfloat16 [2, 3072, 768], P(None, 'fsdp'), may hold values from -0.15625 to 0.15625
- ffn_out_bias: bfloat16 [2, 768], P(None, 'fsdp'), may hold values from -3 to 3
- norm_gain: bfloat16 [5, 768], P(None, 'fsdp'), may hold values from 0.5 to 1.5
- norm_bias: bfloat16 [5, 768], P(None, 'fsdp'), may hold values from -2 to 2
- word_cot: bfloat16 [128, 20, 768], P(('dp', 'fsdp')), may hold values from -6 to 6
- region_cot: bfloat16 [128, 36, 768], P(('dp', 'fsdp')), may hold values from -6 to 6
Outputs:
- lang_out: bfloat16 [128, 20, 768], P(('dp', 'fsdp'))
- vis_out: bfloat16 [128, 36, 768], P(('dp', 'fsdp'))
- words_grad: float32 [128, 20, 768], P(('dp', 'fsdp'))
- regions_grad: float32 [128, 36, 768], P(('dp', 'fsdp'))
- attn_qkv_grad: float32 [3, 3, 768, 768], P(None, None, 'fsdp')
- attn_out_grad: float32 [3, 768, 768], P(None, 'fsdp')
- attn_bias_grad: float32 [3, 3, 768], P(None, None, 'fsdp')
- ffn_in_grad: float32 [2, 768, 3072], P(None, 'fsdp')
- ffn_in_bias_grad: float32 [2, 3072], P(None, 'fsdp')
- ffn_out_grad: float32 [2, 3072, 768], P(None, 'fsdp')
- ffn_out_bias_grad: float32 [2, 768], P(None, 'fsdp')
- norm_gain_grad: float32 [5, 768], P(None, 'fsdp')
- norm_bias_grad: float32 [5, 768], P(None, 'fsdp')
The draws below stay inside these ranges and needn't reach their ends.
Inputs may be any that keep to these rules, and one draw needn't show every extreme that they name: Each item's first word_count words are live, the rest of its 20 slots are padding. Each item's first region_count regions are live, the rest of its 36 slots are padding.
All inputs are finite; a program needn't handle non-finite values.
Results may differ from the reference program's by a relative error of at most 0.024.
Values may be sent and summed in bfloat16 or wider, within the bound.
A program may use at most 256 MiB of HBM per device.

```python
import jax
import jax.numpy as jnp
from jax import lax

D = 768
FF = 3072
HEADS = 12
HEAD_DIM = 64
WORDS = 20
REGIONS = 36
ITEMS_DEV = 4
ITEMS = 128


def draw_word_count(key, part):
    key_first, key_second, key_full = jax.random.split(jax.random.fold_in(key, 11), 3)
    first_draw = jax.random.randint(key_first, (ITEMS,), 0, WORDS - 4)
    second_draw = jax.random.randint(key_second, (ITEMS,), 0, WORDS - 4)
    counts = 5 + jnp.minimum(first_draw, second_draw)
    full_item = jax.random.randint(key_full, (), 0, ITEMS)
    return jnp.where(jnp.arange(ITEMS) == full_item, WORDS, counts).astype(jnp.int32)


def draw_region_count(key, part):
    key_first, key_second, key_third, key_full = jax.random.split(jax.random.fold_in(key, 23), 4)
    first_draw = jax.random.randint(key_first, (ITEMS,), 0, REGIONS - 9)
    second_draw = jax.random.randint(key_second, (ITEMS,), 0, REGIONS - 9)
    third_draw = jax.random.randint(key_third, (ITEMS,), 0, REGIONS - 9)
    counts = 10 + jnp.minimum(jnp.minimum(first_draw, second_draw), third_draw)
    full_item = jax.random.randint(key_full, (), 0, ITEMS)
    return jnp.where(jnp.arange(ITEMS) == full_item, REGIONS, counts).astype(jnp.int32)


def levels(stream_key, shape, cuts, least, top_value):
    factor_of, own = 1.0, jax.random.fold_in(stream_key, 6)
    for axis_at, blocks in cuts:
        heights = jnp.exp(jax.random.uniform(jax.random.fold_in(own, axis_at), (blocks,), jnp.float32, least / len(cuts), top_value / len(cuts)))
        factor_of = factor_of * jnp.repeat(heights, shape[axis_at] // blocks).reshape([-1 if axis == axis_at else 1 for axis in range(len(shape))])
    return factor_of


def noise(stream_key, dims, deviation, limit, cuts=(), kind=jnp.bfloat16):
    array = deviation * jax.random.normal(stream_key, dims, jnp.float32)
    if cuts:
        array = array * levels(stream_key, dims, cuts, -0.22, 0.18)
    return jnp.clip(array, -limit, limit).astype(kind)


def setup_inputs(seed: int = 0) -> dict:
    key_list = jax.random.split(jax.random.key(seed), 16)
    return {
        "words": noise(key_list[0], (ITEMS, WORDS, D), 1.0, 6.0, ((0, 32),)),
        "regions": noise(key_list[1], (ITEMS, REGIONS, D), 1.0, 6.0, ((0, 32),)),
        "word_count": draw_word_count(jax.random.fold_in(key_list[15], 71), 0),
        "region_count": draw_region_count(jax.random.fold_in(key_list[15], 71), 0),
        "attn_qkv": noise(key_list[4], (3, 3, D, D), D ** -0.5, 0.21875, ((2, 8),)),
        "attn_out": noise(key_list[5], (3, D, D), (D // 8) ** -0.5, 0.625, ((1, 8),)),
        "attn_bias": noise(key_list[6], (3, 3, D), 0.5, 3.0, ((2, 8),)),
        "ffn_in": noise(key_list[7], (2, D, FF), D ** -0.5, 0.21875, ((1, 8),)),
        "ffn_in_bias": noise(key_list[8], (2, FF), 0.5, 3.0, ((1, 8),)),
        "ffn_out": noise(key_list[9], (2, FF, D), (FF // 2) ** -0.5, 0.15625, ((1, 8),)),
        "ffn_out_bias": noise(key_list[10], (2, D), 0.5, 3.0, ((1, 8),)),
        "norm_gain": jnp.clip(1.0 + 0.1 * jax.random.normal(key_list[11], (5, D), jnp.float32), 0.5, 1.5).astype(jnp.bfloat16),
        "norm_bias": noise(key_list[12], (5, D), 0.3, 2.0, ((1, 8),)),
        "word_cot": noise(key_list[13], (ITEMS, WORDS, D), 1.0, 6.0, ((0, 32),)),
        "region_cot": noise(key_list[14], (ITEMS, REGIONS, D), 1.0, 6.0, ((0, 32),)),
    }


EPS = 1e-06
NEG = -1e+30
HIGH = lax.Precision.HIGHEST

@jax.custom_vjp
def low(v):
    return lax.optimization_barrier(v.astype(jnp.bfloat16)).astype(jnp.float32)

@jax.custom_vjp
def low_back(v):
    return v

def low_keep(v):
    return (low(v), None)

def low_pass(kept, grad):
    return (grad,)

def back_keep(v):
    return (v, None)

def back_low(kept, grad):
    return (low(grad),)
low.defvjp(low_keep, low_pass)
low_back.defvjp(back_keep, back_low)

def layer_norm(inputs, norm_scale, norm_shift):
    centered = inputs - lax.optimization_barrier(jnp.mean(inputs, -1, keepdims=True))
    spread = lax.rsqrt(lax.optimization_barrier(jnp.mean(centered * centered, -1, keepdims=True)) + EPS)
    return centered * spread * norm_scale + norm_shift

def project(rows, weight):
    return low_back(jnp.einsum('nld,de->nle', rows, weight, precision=HIGH))

def split_heads(inputs):
    return inputs.reshape(inputs.shape[0], inputs.shape[1], HEADS, HEAD_DIM)

def attend(query_rows, key_rows, key_live, weight_three, out_weight, offsets):
    queries = split_heads(low(project(query_rows, weight_three[0]) + offsets[0]))
    keys_low = split_heads(low(project(key_rows, weight_three[1])))
    values_low = split_heads(low(project(key_rows, weight_three[2]) + offsets[1]))
    scores = low_back(jnp.einsum('nqhe,nkhe->nhqk', queries, keys_low, precision=HIGH) * HEAD_DIM ** (-0.5))
    scores = jnp.where(key_live[:, None, None, :], scores, NEG)
    weights = low(jax.nn.softmax(scores, axis=-1))
    context = low(low_back(jnp.einsum('nhqk,nkhe->nqhe', weights, values_low, precision=HIGH)))
    context = context.reshape(query_rows.shape[0], query_rows.shape[1], HEADS * HEAD_DIM)
    return project(context, out_weight) + offsets[2]

def feed_forward(stream, weight_in, offset_in, weight_out, offset_out):
    hidden = jax.nn.gelu(project(low(stream), weight_in) + offset_in, approximate=False)
    return project(low(hidden), weight_out) + offset_out

def layer(params, words, regions, word_live, region_live):
    attn_qkv, attn_out, attn_bias, ffn_in, ffn_in_bias, ffn_out, ffn_out_bias, norm_gain, norm_bias = params
    lang_one = layer_norm(words + attend(words, regions, region_live, attn_qkv[0], attn_out[0], attn_bias[0]), norm_gain[0], norm_bias[0])
    vis_one = layer_norm(regions + attend(regions, words, word_live, attn_qkv[0], attn_out[0], attn_bias[0]), norm_gain[0], norm_bias[0])
    lang_low = low(lang_one)
    lang_two = layer_norm(lang_one + attend(lang_low, lang_low, word_live, attn_qkv[1], attn_out[1], attn_bias[1]), norm_gain[1], norm_bias[1])
    vis_low = low(vis_one)
    vis_two = layer_norm(vis_one + attend(vis_low, vis_low, region_live, attn_qkv[2], attn_out[2], attn_bias[2]), norm_gain[2], norm_bias[2])
    lang_three = layer_norm(lang_two + feed_forward(lang_two, ffn_in[0], ffn_in_bias[0], ffn_out[0], ffn_out_bias[0]), norm_gain[3], norm_bias[3])
    vis_three = layer_norm(vis_two + feed_forward(vis_two, ffn_in[1], ffn_in_bias[1], ffn_out[1], ffn_out_bias[1]), norm_gain[4], norm_bias[4])
    return (lang_three, vis_three)

def widen(array_in):
    return array_in.astype(jnp.float32)

def reference(words, regions, word_count, region_count, attn_qkv, attn_out, attn_bias, ffn_in, ffn_in_bias, ffn_out, ffn_out_bias, norm_gain, norm_bias, word_cot, region_cot):
    params = jax.tree.map(widen, (attn_qkv, attn_out, attn_bias, ffn_in, ffn_in_bias, ffn_out, ffn_out_bias, norm_gain, norm_bias))
    block_items = 2 * ITEMS_DEV
    block_count = ITEMS // block_items

    def fold(array_in):
        return array_in.reshape((block_count, block_items) + array_in.shape[1:])
    pieces_all = (fold(words), fold(regions), fold(word_count), fold(region_count), fold(word_cot), fold(region_cot))

    def one_block(totals, pieces):
        word_rows, region_rows, word_lengths, region_lengths, word_cot_block, region_cot_block = pieces
        word_live = jnp.arange(WORDS, dtype=jnp.int32)[None, :] < word_lengths[:, None]
        region_live = jnp.arange(REGIONS, dtype=jnp.int32)[None, :] < region_lengths[:, None]

        def forward(weights_all, lang_in, vis_in):
            return layer(weights_all, lang_in, vis_in, word_live, region_live)
        outputs, pull = jax.vjp(forward, params, word_rows.astype(jnp.float32), region_rows.astype(jnp.float32))
        lang_cot = jnp.where(word_live[:, :, None], word_cot_block.astype(jnp.float32), 0.0)
        vis_cot = jnp.where(region_live[:, :, None], region_cot_block.astype(jnp.float32), 0.0)
        weight_grads, lang_grad, vis_grad = pull((lang_cot, vis_cot))
        totals = jax.tree.map(jnp.add, totals, weight_grads)
        return (totals, (outputs[0].astype(jnp.bfloat16), outputs[1].astype(jnp.bfloat16), lang_grad, vis_grad))
    totals, results = lax.scan(one_block, jax.tree.map(jnp.zeros_like, params), pieces_all)

    def unfold(array_in):
        return array_in.reshape((ITEMS,) + array_in.shape[2:])
    return (unfold(results[0]), unfold(results[1]), unfold(results[2]), unfold(results[3]), totals[0], totals[1], totals[2], totals[3], totals[4], totals[5], totals[6], totals[7], totals[8])
```

```python
import functools
import math
from types import SimpleNamespace

import jax
import jax.numpy as jnp
from jax import lax
from jax.experimental import pallas as pl
from jax.experimental.pallas import tpu as pltpu
from jax.sharding import PartitionSpec as P

HEADS = 12
HEAD_DIM = 64
EPS = 1e-06
NEG = -1e30
OUTER = 4
VECTORS = 24
AHEAD = 3
BF16 = jnp.bfloat16
F32 = jnp.float32
MESH = pl.DeviceIdType.MESH
S = (0, 1)
NN = ((1,), (0,))
NT = ((1,), (1,))
TN = ((0,), (0,))


def window(size, devices):
    worst = max((size * f) % 128 for f in range(devices))
    return -(-(size + worst) // 128) * 128


def al(value, step=128):
    return pl.multiple_of(value, step)


def rcopy(src, dst, send, recv, device):
    return pltpu.make_async_remote_copy(
        src_ref=src, dst_ref=dst, send_sem=send, recv_sem=recv, device_id=device, device_id_type=MESH
    )


def dot(a, b, dims):
    return lax.dot_general(a, b, (dims, ((), ())), preferred_element_type=F32)


def spaces(tree):
    if isinstance(tree, dict):
        return SimpleNamespace(**{k: spaces(v) for k, v in tree.items()})
    if isinstance(tree, list):
        return [spaces(v) for v in tree]
    return tree


def tiles(count, body):
    def run(t, carry):
        body(t)
        return carry

    lax.fori_loop(0, count, run, 0)


def add_rows(into, terms, rows, fresh=False):
    step = 32 if rows % 32 == 0 else 16 if rows % 16 == 0 else 8

    def body(i):
        at = pl.ds(al(i * step, step), step)
        value = None if fresh else into[at, :].astype(F32)
        for term in terms:
            more = term[at, :].astype(F32)
            value = more if value is None else value + more
        into[at, :] = value.astype(BF16)

    tiles(rows // step, body)


class Place:
    def __init__(self, fsdp):
        self.A, self.F = OUTER, fsdp
        self.B = fsdp // OUTER
        r, f = lax.axis_index("dp"), lax.axis_index("fsdp")
        self.r, self.f = r, f
        self.c, self.y = lax.rem(r, 2), lax.rem(r // 2, 2)
        self.o, self.b = f // self.B, lax.rem(f, self.B)
        self.core_peer = (r + 1 - 2 * self.c, f)
        self.y_peer = (r + 2 - 4 * self.y, f)
        self.far_peer = (r + 3 - 4 * self.y - 2 * self.c, f)

    def out_at(self, o):
        return (self.r, o * self.B + self.b)

    def out_peer(self, d):
        return self.out_at(lax.rem(self.o + d, self.A))

    def in_peer(self, d):
        return (self.r, self.o * self.B + lax.rem(self.b + d, self.B))

    def peers(self):
        return (
            [self.core_peer, self.y_peer, self.far_peer]
            + [self.out_peer(d) for d in range(1, self.A)]
            + [self.in_peer(d) for d in range(1, self.B)]
        )


class Ways:
    def __init__(self, outer, middle, step=128):
        self.outer, self.middle, self.step = outer, middle, step

    def own(self, y):
        at = y * (self.outer + self.middle)
        return (al(at, self.step) if self.step > 1 else at), self.outer

    def both(self):
        return self.outer, self.middle

    def other(self, y):
        return self.own(1 - y)


class Tensor:
    def __init__(self, g, t, src, view, rows, half, ways, sems, bufs, out, whole=None):
        self.g, self.t, self.src, self.view, self.whole = g, t, src, view, whole
        self.rs, self.split, self.ways, self.sems, self.bufs, self.out = rows, half, ways, sems, bufs, out
        self.private = whole is None
        self.qs = (1,) if self.private else (0, 1)
        self.stages = 3 if self.private else 6

    def sem(self, array, *at):
        return array.at[(self.t, *at)]

    def keys(self):
        g = self.g
        if self.split:
            return [(k, g.c * (g.A // 2) + k) for k in range(g.A // 2)]
        return [(d, lax.rem(g.o + g.A - d, g.A)) for d in (0, 2, 3, 1)[: g.A]]

    def row(self, o, b):
        g = self.g
        at = (o * g.B + b) * self.rs
        if self.split:
            at = lax.rem(at, (g.F // 2) * self.rs)
        return al(at, 8)

    def inset(self):
        return self.g.o // (self.g.A // 2) == self.g.c

    def mine(self, fn):
        if self.split:
            pl.when(self.inset())(fn)
        else:
            fn()

    def others(self, fn):
        if self.split:
            pl.when(jnp.logical_not(self.inset()))(fn)
        else:
            fn()

    def cols(self, q, back=False):
        way = self.ways
        return way.own(self.g.y) if q == 0 else way.both()

    def part(self, q, o, b, back=False):
        return self.view(self.row(o, b), self.rs, *self.cols(q, back))


    def own_copy(self, q):
        g = self.g
        return pltpu.make_async_copy(
            self.src(*self.cols(q)), self.part(q, g.o, g.b), self.sem(self.sems.own, q)
        )

    def zcopy(self, q, d):
        g = self.g
        slot = lax.rem(g.o, g.A // 2) if self.split else d - 1
        return rcopy(
            self.src(*self.cols(q)),
            self.part(q, g.o, g.b),
            self.sem(self.sems.zs, q, d - 1),
            self.sem(self.sems.zr, q, slot),
            g.out_peer(d),
        )

    def xcopy(self, q, d, k, o, from_src=False):
        g = self.g
        v = self.part(q, o, g.b)
        i = (d - 1) * g.A + k
        return rcopy(
            self.src(*self.cols(q)) if from_src else v,
            v,
            self.sem(self.sems.xs, q, i),
            self.sem(self.sems.xr, q, i),
            g.in_peer(d),
        )

    def ycopy(self, k, o):
        g = self.g
        v = self.view(self.row(o, 0), self.rs * g.B, *self.cols(0))
        return rcopy(v, v, self.sem(self.sems.ys, k), self.sem(self.sems.yr, k), g.y_peer)

    def own_slot(self):
        return lax.rem(self.g.o, self.g.A // 2) if self.split else 0

    def start_z(self):
        def go():
            for q in self.qs:
                for d in (2, 3, 1)[: self.g.A - 1]:
                    self.zcopy(q, d).start()

        self.mine(go)

    def start_x(self):
        g = self.g

        def go():
            for q in self.qs:
                self.own_copy(q).start()
                for d in range(1, g.B):
                    self.xcopy(q, d, self.own_slot(), g.o, True).start()

        self.mine(go)

    def forward_x(self):
        g = self.g
        for q in self.qs:
            for k, o in self.keys():

                def go(k=k, o=o, q=q):
                    v = self.part(q, o, g.b)
                    slot = k if self.split else k - 1
                    rcopy(
                        v, v, self.sem(self.sems.zs, q, 0), self.sem(self.sems.zr, q, slot), g.out_peer(1)
                    ).wait_recv()
                    for d in range(1, g.B):
                        self.xcopy(q, d, k, o).start()

                if self.split:
                    pl.when(o != g.o)(go)
                elif k > 0:
                    go()

    def x_arrived(self, q, k, o):
        g = self.g
        for d in range(1, g.B):
            v = self.part(q, o, lax.rem(g.b + g.B - d, g.B))
            i = (d - 1) * g.A + k
            rcopy(v, v, self.sem(self.sems.xs, q, i), self.sem(self.sems.xr, q, i), g.in_peer(1)).wait_recv()

    def forward_y0(self):
        g = self.g

        def go():
            k = self.own_slot()
            self.own_copy(0).wait()
            self.x_arrived(0, k, g.o)
            self.ycopy(k, g.o).start()

        self.mine(go)

    def forward_y(self):
        g = self.g
        for k, o in self.keys():

            def go(k=k, o=o):
                self.x_arrived(0, k, o)
                self.ycopy(k, o).start()

            if self.split:
                pl.when(o != g.o)(go)
            elif k > 0:
                go()

    def arrived(self):
        g = self.g
        self.mine(lambda: self.own_copy(1).wait())
        for k, o in self.keys():
            self.x_arrived(1, k, o)
            if not self.private:
                v = self.view(self.row(o, 0), self.rs * g.B, *self.ways.other(g.y))
                rcopy(v, v, self.sem(self.sems.ys, k), self.sem(self.sems.yr, k), g.y_peer).wait_recv()

    def drain(self):
        g = self.g

        def go():
            for q in self.qs:
                for d in range(1, g.A):
                    self.zcopy(q, d).wait_send()

        self.mine(go)
        for k, o in self.keys():
            for q in self.qs:
                for d in range(1, g.B):
                    self.xcopy(q, d, k, o).wait_send()
            if not self.private:
                self.ycopy(k, o).wait_send()


    def total_rows(self):
        return self.rs * (self.g.F // 2 if self.split else self.g.F)

    def owners(self):
        g = self.g
        if self.split:
            return [(k, g.c * (g.A // 2) + k) for k in range(g.A // 2)]
        return [(d, lax.rem(g.o + d, g.A)) for d in (2, 3, 1, 0)]

    def back_y(self):
        g = self.g
        v = self.view(0, self.total_rows(), *self.ways.other(g.y))
        return rcopy(v, self.bufs.y, self.sem(self.sems.gys), self.sem(self.sems.gyr), g.y_peer)

    def back_x(self, q, d, k, o, b):
        g = self.g
        i = (d - 1) * g.A + k
        return rcopy(
            self.part(q, o, b, True),
            self.bufs.x[q].at[i],
            self.sem(self.sems.gxs, q, i),
            self.sem(self.sems.gxr, q, i),
            g.in_peer(d),
        )

    def back_z(self, q, k, o):
        g = self.g
        slot = lax.rem(o - g.o + g.A, g.A) - 1 if self.split else k - 1
        return rcopy(
            self.part(q, o, g.b, True),
            self.bufs.z[q].at[slot],
            self.sem(self.sems.gzs, q, k if self.split else k - 1),
            self.sem(self.sems.gzr, q, slot),
            g.out_at(o),
        )

    def each_z(self, q, k, o, way):
        if self.split:
            pl.when(o != self.g.o)(lambda: way(self.back_z(q, k, o)))
        elif k > 0:
            way(self.back_z(q, k, o))

    def back_y2(self, q):
        g = self.g
        return rcopy(
            self.part(q, g.o, g.b, True),
            self.bufs.y2[q],
            self.sem(self.sems.gws, q),
            self.sem(self.sems.gwr, q),
            g.y_peer,
        )

    def back_core(self):
        g = self.g
        return rcopy(
            self.whole(self.row(g.o, g.b), self.rs),
            self.bufs.c,
            self.sem(self.sems.gcs),
            self.sem(self.sems.gcr),
            g.core_peer,
        )

    def put_own(self):
        g = self.g
        return pltpu.make_async_copy(
            self.whole(self.row(g.o, g.b), self.rs), self.out(g.c), self.sem(self.sems.put, 0)
        )

    def put_other(self):
        return pltpu.make_async_copy(self.bufs.c, self.out(1 - self.g.c), self.sem(self.sems.put, 1))

    def fin(self, i):
        g = self.g
        return rcopy(
            self.part(1, g.o, g.b),
            self.bufs.fin.at[i],
            self.sem(self.sems.fs, i),
            self.sem(self.sems.fr, i),
            (g.core_peer, g.y_peer, g.far_peer)[i],
        )

    def put(self, i):
        g = self.g
        c = (1 - g.c, g.c, 1 - g.c, g.c)[i]
        y = (g.y, 1 - g.y, 1 - g.y, g.y)[i]
        source = self.part(1, g.o, g.b) if i == 3 else self.bufs.fin.at[i]
        return pltpu.make_async_copy(source, self.out(y, c), self.sem(self.sems.put, i))

    def taken(self):
        return ((1,), (0, 2)) if self.split else ((0, 1, 2), ())

    def send(self):
        if not self.private:
            self.back_y().start()
        self.send_x(1)

    def send_x(self, q, only=None):
        g = self.g
        for k, o in self.owners():
            if only is None or k == only:
                for d in range(1, g.B):
                    self.back_x(q, d, k, o, lax.rem(g.b + d, g.B)).start()

    def take_y(self):
        self.back_y().wait_recv()
        rows = self.total_rows()
        add_rows(self.view(0, rows, *self.cols(0, True)), [self.bufs.y], rows)
        self.send_x(0)

    def take_x(self, q):
        g = self.g
        for k, o in self.owners():
            terms = []
            for d in range(1, g.B):
                self.back_x(q, d, k, o, g.b).wait_recv()
                terms.append(self.bufs.x[q].at[(d - 1) * g.A + k])
            if terms:
                add_rows(self.part(q, o, g.b, True), terms, self.rs)
            self.each_z(q, k, o, lambda copy: copy.start())

    def take_z(self, q):
        g = self.g

        def go():
            v = self.part(q, g.o, g.b, True)
            for d in range(g.A - 1):
                rcopy(
                    v,
                    self.bufs.z[q].at[d],
                    self.sem(self.sems.gzs, q, 0),
                    self.sem(self.sems.gzr, q, d),
                    g.out_peer(1),
                ).wait_recv()
            add_rows(v, [self.bufs.z[q].at[d] for d in range(g.A - 1)], self.rs)
            if self.private:
                for i in range(3):
                    self.fin(i).start()
                self.put(3).start()
            else:
                self.back_y2(q).start()

        self.mine(go)

    def take_y2(self, q):
        g = self.g

        def go():
            self.back_y2(q).wait()
            if q == 1:
                add_rows(self.part(1, g.o, g.b, True), [self.bufs.y2[1]], self.rs)
            else:
                self.back_y().wait_send()
                at = self.view(self.row(g.o, g.b), self.rs, *self.ways.other(g.y))
                add_rows(at, [self.bufs.y2[0]], self.rs, fresh=True)
                self.back_core().start()
                self.put_own().start()

        self.mine(go)
        if q == 0 and self.split:
            self.others(lambda: self.back_y().wait_send())

    def take_core(self):
        def go():
            self.back_core().wait_recv()
            self.put_other().start()

        self.others(go)

    def take_fin(self):
        def go(which):
            for i in which:
                self.fin(i).wait_recv()
                self.put(i).start()

        self.mine(lambda: go(self.taken()[0]))
        self.others(lambda: go(self.taken()[1]))

    def stage(self, n):
        if self.private:
            if n == 0:
                self.take_x(1)
            elif n == 1:
                self.take_z(1)
            elif n == 2:
                self.take_fin()
        elif n == 0:
            self.take_y()
        elif n == 1:
            self.take_x(1)
        elif n == 2:
            self.take_x(0)
            self.take_z(1)
        elif n == 3:
            self.take_z(0)
            self.take_y2(1)
        elif n == 4:
            self.take_y2(0)
        elif n == 5:
            self.take_core()

    def finish(self):
        g = self.g
        for q in self.qs:
            for d in range(1, g.B):
                for k, o in self.owners():
                    self.back_x(q, d, k, o, g.b).wait_send()
            for k, o in self.owners():
                self.each_z(q, k, o, lambda copy: copy.wait_send())

        def mine():
            if self.private:
                for i in range(3):
                    self.fin(i).wait_send()
                for i in self.taken()[0] + (3,):
                    self.put(i).wait()
            else:
                self.back_core().wait_send()
                self.put_own().wait()

        def others():
            if self.private:
                for i in self.taken()[1]:
                    self.put(i).wait()
            else:
                self.put_other().wait()

        self.mine(mine)
        self.others(others)


def kernel(tree, sizes, *refs):
    inp, out, R = (spaces(part) for part in jax.tree.unflatten(tree, refs))
    F, D, FF, n, items = sizes
    g = Place(F)
    h, hf = D // 2, FF // 2
    scale = HEAD_DIM ** (-0.5)
    pairs = HEADS // 4
    sems = R.sem

    meet = pltpu.get_barrier_semaphore()
    peers = g.peers()
    for peer in peers:
        pl.semaphore_signal(meet, inc=1, device_id=peer, device_id_type=MESH)
    pl.semaphore_wait(meet, len(peers))

    rs, rf = D // F, FF // F
    line = []

    def make(*args):
        line.append(Tensor(g, len(line), *args))
        return line[-1]

    q0 = make(
        lambda j, k: inp.attn_qkv.at[0, j, :, pl.ds(al(g.c * h), h)],
        lambda r, k, j, kj: R.wq0.at[j, pl.ds(r, k), :],
        rs,
        False,
        Ways(1, 1, 1),
        sems,
        R.gq0,
        lambda c: out.q.at[0, :, :, pl.ds(al(c * h), h)],
        lambda r, k: R.wq0.at[:, pl.ds(r, k), :],
    )
    o0 = make(
        lambda j, k: inp.attn_out.at[0, :, pl.ds(j, k)],
        lambda r, k, j, kj: R.wo0.at[pl.ds(r, k), pl.ds(j, kj)],
        rs,
        True,
        Ways(D // 3, D // 3),
        sems,
        R.go0,
        lambda c: out.o.at[0],
        lambda r, k: R.wo0.at[pl.ds(r, k), :],
    )
    qp = [
        make(
            lambda j, k, i=i: inp.attn_qkv.at[1 + g.y, i, :, pl.ds(al(g.c * h), h)],
            lambda r, k, j, kj, i=i: R.wq.at[i, pl.ds(r, k), :],
            rs,
            False,
            Ways(0, h),
            sems,
            R.gq[i],
            lambda y, c, i=i: out.q.at[1 + y, i, :, pl.ds(al(c * h), h)],
        )
        for i in range(3)
    ]
    op = make(
        lambda j, k: inp.attn_out.at[1 + g.y],
        lambda r, k, j, kj: R.wo.at[pl.ds(r, k), :],
        rs,
        True,
        Ways(0, D),
        sems,
        R.go,
        lambda y, c: out.o.at[1 + y],
    )
    wide, long = hf // 2, D // 2
    ip = [
        make(
            lambda j, k, i=i: inp.ffn_in.at[g.y, :, pl.ds(al(g.c * hf + i * wide), wide)],
            lambda r, k, j, kj, i=i: R.wi.at[pl.ds(r, k), pl.ds(i * wide, wide)],
            rs,
            False,
            Ways(0, wide),
            sems,
            R.gi[i],
            lambda y, c, i=i: out.i.at[y, :, pl.ds(al(c * hf + i * wide), wide)],
        )
        for i in range(2)
    ]
    fp = [
        make(
            lambda j, k, i=i: inp.ffn_out.at[g.y, :, pl.ds(i * long, long)],
            lambda r, k, j, kj, i=i: R.wf.at[pl.ds(r, k), pl.ds(i * long, long)],
            rf,
            True,
            Ways(0, long),
            sems,
            R.gf[i],
            lambda y, c, i=i: out.f.at[y, :, pl.ds(i * long, long)],
        )
        for i in range(2)
    ]

    slot_of = lambda f: R.vec_in.at[f]

    def vec_z(d):
        return rcopy(inp.vectors, slot_of(g.f), sems.vzs.at[d - 1], sems.vzr.at[d - 1], g.out_peer(d))

    def vec_x(d, k):
        o = lax.rem(g.o + g.A - k, g.A)
        at = slot_of(o * g.B + g.b)
        i = (d - 1) * g.A + k
        return rcopy(inp.vectors if k == 0 else at, at, sems.vxs.at[i], sems.vxr.at[i], g.in_peer(d))

    for d in range(1, g.A):
        vec_z(d).start()
    for d in range(1, g.B):
        vec_x(d, 0).start()

    count = [0, 0]

    def exchange(src, dst, device=None, start=True):
        i = count[0]
        count[0] += 1
        copy = rcopy(src, dst, sems.es.at[i], sems.er.at[i], g.core_peer if device is None else device)
        if start:
            copy.start()
        return copy

    def load(src, dst, start=True):
        i = count[1]
        count[1] += 1
        copy = pltpu.make_async_copy(src, dst, sems.load.at[i])
        if start:
            copy.start()
        return copy

    def this(s):
        return g.y == s

    def that(s):
        return g.y != s

    x0_own = [load(inp.x[s], R.x0[s].at[pl.ds(0, n[s])]) for s in S]
    x0_other = [exchange(inp.x[s], R.x0[s].at[pl.ds(n[s], n[s])]) for s in S]

    def item_of(at, slots):
        return sum((at >= slots * i).astype(jnp.int32) for i in range(1, items))

    lane = lax.broadcasted_iota(jnp.int32, (8, 128 + n[1]), 1)
    slots = [n[s] // items for s in S]
    alive = jnp.zeros((8, 128 + n[1]), jnp.int32)
    for s in S:
        for i in range(items):
            start = 128 * s + slots[s] * i
            alive = alive + ((lane >= start) & (lane < start + inp.live[s][i])).astype(jnp.int32)
    R.keys[0] = jnp.where(alive > 0, 0.0, NEG)
    key_other = [
        exchange(R.keys.at[0], R.keys.at[i], device)
        for i, device in ((2, g.core_peer), (1, g.y_peer), (3, g.far_peer))
    ]
    vec_own = load(inp.vectors, slot_of(g.f))
    q0.start_z()
    q0.start_x()
    o0.start_z()
    o0.start_x()
    line[2].start_z()
    line[2].start_x()
    for x in line[3:]:
        x.start_z()
    cot_own = [load(inp.cot[s], R.cot.at[pl.ds(0, n[s])], False) for s in S]
    cot_other = [exchange(inp.cot[s], R.cot.at[pl.ds(n[s], n[s])], g.y_peer, False) for s in S]
    for s in S:
        pl.when(this(s))(cot_own[s].start)
        pl.when(that(s))(cot_other[s].start)

    for k in range(1, g.A):
        o = lax.rem(g.o + g.A - k, g.A)
        at = slot_of(o * g.B + g.b)
        rcopy(at, at, sems.vzs.at[0], sems.vzr.at[k - 1], g.out_peer(1)).wait_recv()
        for d in range(1, g.B):
            vec_x(d, k).start()
    for d in range(1, g.B):
        for k in range(g.A):
            o = lax.rem(g.o + g.A - k, g.A)
            at = slot_of(o * g.B + lax.rem(g.b + g.B - d, g.B))
            i = (d - 1) * g.A + k
            rcopy(at, at, sems.vxs.at[i], sems.vxr.at[i], g.in_peer(1)).wait_recv()
    vec_own.wait()
    vec, vin, grad = R.vec, R.vin, R.grad
    vec[...] = jnp.zeros_like(vec)
    vin[...] = jnp.zeros_like(vin)
    grad[...] = jnp.zeros_like(grad)
    for f in range(F):
        for into, low, high, size in ((vec, 0, VECTORS, D // F), (vin, VECTORS, VECTORS + 8, FF // F)):
            start, turn, span = size * f // 128 * 128, size * f % 128, window(size, F)
            piece = R.vec_in[f, low:high, 0:span].astype(F32)
            into[:, start : start + span] += pltpu.roll(piece, turn, 1) if turn else piece

    def row_of(i):
        return vec[i : i + 1, 0:D]

    ATT_BIAS, OUT_BIAS, GAIN, SHIFT = 0, 9, 11, 16

    for copy in key_other:
        copy.wait_recv()

    def build(b):
        lane = lax.broadcasted_iota(jnp.int32, (1, 128 + n[1]), 1)
        key_item = jnp.where(lane < 128, item_of(lane, n[0] // items), item_of(lane - 128, n[1] // items))
        for s in S:
            query_item = item_of(lax.broadcasted_iota(jnp.int32, (n[s], 1), 0), n[s] // items)
            rows = pl.ds(s * n[0], n[s])
            R.masks[b, rows, :] = jnp.where(query_item == key_item, R.keys[b, 0:1, :], NEG)

    tiles(4, build)
    for s in S:
        x0_own[s].wait()
    for s in S:
        x0_other[s].wait_recv()

    def project(m, x, wq, qkv):
        for j in range(3):
            value = dot(x[...], wq[j], NN)
            if j != 1:
                row = ATT_BIAS + 3 * m + (0 if j == 0 else 1)
                value = value + vec[row : row + 1, pl.ds(al(g.c * h), h)]
            qkv[j] = value.astype(BF16)

    def mask_of(b, qs, ks):
        return R.masks[b, pl.ds(qs * n[0], n[qs]), pl.ds(ks * 128, n[ks])]

    def attend(qs, ks, q_ref, kv_ref, probs, context, total):
        def body(b):
            qr, kr = pl.ds(al(b * n[qs], 16), n[qs]), pl.ds(al(b * n[ks], 16), n[ks])
            mask = mask_of(b * (4 // total), qs, ks)
            cut = lambda ref, j, rows, i: ref[j, rows, i * HEAD_DIM : (i + 1) * HEAD_DIM]
            heads = range(2 * pairs)
            scores = [dot(cut(q_ref, 0, qr, i), cut(kv_ref, 1, kr, i), NT) * scale + mask for i in heads]
            tops = [jnp.max(v, -1, keepdims=True) for v in scores]
            exs = [jnp.exp(v - top) for v, top in zip(scores, tops)]
            sums = [1.0 / jnp.sum(v, -1, keepdims=True) for v in exs]
            shares = [v * k for v, k in zip(exs, sums)]
            parts = [dot(pr.astype(BF16), cut(kv_ref, 2, kr, i), NN) for i, pr in enumerate(shares)]
            made = [jnp.concatenate(parts[2 * p : 2 * p + 2], 1).astype(BF16) for p in range(pairs)]
            for i, pr in enumerate(shares):
                probs[2 * pairs * b + i, 0 : n[qs], 0 : n[ks]] = pr
            for p, value in enumerate(made):
                context[qr, p * 128 : (p + 1) * 128] = value

        tiles(total, body)

    def attend_back(qs, ks, q_ref, kv_ref, probs, dc_ref, dq_ref, dkv_ref, m, total):
        def body(b):
            qr, kr = pl.ds(al(b * n[qs], 16), n[qs]), pl.ds(al(b * n[ks], 16), n[ks])
            cut = lambda ref, j, rows, i: ref[j, rows, i * HEAD_DIM : (i + 1) * HEAD_DIM]
            heads = range(2 * pairs)
            dcs = [dc_ref[qr, i * HEAD_DIM : (i + 1) * HEAD_DIM] for i in heads]
            prs = [probs[2 * pairs * b + i, 0 : n[qs], 0 : n[ks]] for i in heads]
            dps = [dot(d, cut(kv_ref, 2, kr, i), NT) for i, d in enumerate(dcs)]
            dvs = [dot(pr.astype(BF16), d, TN) for pr, d in zip(prs, dcs)]
            sums = [jnp.sum(pr * dp, -1, keepdims=True) for pr, dp in zip(prs, dps)]
            dss = [(pr * (dp - k)).astype(BF16) for pr, dp, k in zip(prs, dps, sums)]
            dqs = [dot(ds, cut(kv_ref, 1, kr, i), NN) * scale for i, ds in enumerate(dss)]
            dks = [dot(ds, cut(q_ref, 0, qr, i), TN) * scale for i, ds in enumerate(dss)]
            made = [[jnp.concatenate(v[2 * p : 2 * p + 2], 1) for v in (dqs, dks, dvs)] for p in range(pairs)]
            row = ATT_BIAS + 3 * m
            for p, (dq, dk, dv) in enumerate(made):
                cols = slice(p * 128, (p + 1) * 128)
                dq_ref[0, qr, cols] = dq.astype(BF16)
                dkv_ref[1, kr, cols] = dk.astype(BF16)
                dkv_ref[2, kr, cols] = dv.astype(BF16)
            for p, (dq, dk, dv) in enumerate(made):
                lanes = pl.ds(al(g.c * h + p * 128), 128)
                grad[row : row + 1, lanes] += jnp.sum(dq, 0, keepdims=True)
                grad[row + 1 : row + 2, lanes] += jnp.sum(dv, 0, keepdims=True)

        tiles(total, body)

    def halves(acc, sb, rb, product, step=256):
        rows = acc.shape[0]

        def body(t):
            cols = pl.ds(al(t * step), step)
            value = product(cols)
            acc[:, cols] = value[:rows]
            sb[:, cols] = value[rows:].astype(BF16)

        tiles(D // step, body)
        return exchange(sb, rb)

    def block(rows):
        return next(k for k in (48, 80, 32, 16) if rows % k == 0)

    def norm(base, acc, rb, xh, rr, k, bias, into):
        step = block(acc.shape[0])

        def body(i):
            at = pl.ds(al(i * step, 16), step)
            total = base(at) + ((acc[at, :] + rb[at, :].astype(F32)) + row_of(bias))
            centered = total - jnp.mean(total, -1, keepdims=True)
            spread = lax.rsqrt(jnp.mean(centered * centered, -1, keepdims=True) + EPS)
            xhat = centered * spread
            xh[at, :] = xhat
            rr[at, :] = jnp.broadcast_to(spread, (step, 128))
            into[at, :] = (xhat * row_of(GAIN + k) + row_of(SHIFT + k)).astype(BF16)

        tiles(acc.shape[0] // step, body)

    def norm_back(dy_of, ds, xh, rr, k, bias, f):
        rows = ds.shape[0]
        step = block(rows)

        def body(i, carry):
            at = pl.ds(al(i * step, 16), step)
            dy = dy_of(at)
            xhat = xh[at, :]
            dx = dy * row_of(GAIN + k)
            dyx = dy * xhat
            mean_dx = jnp.mean(dx, -1, keepdims=True)
            mean_dxx = jnp.mean(dx * xhat, -1, keepdims=True)
            dh = rr[at, 0:1] * (dx - mean_dx - xhat * mean_dxx)
            ds[at, :] = dh
            f[at, :] = dh.astype(BF16)
            fold = lambda v: sum(v[j : j + 8] for j in range(0, step, 8))
            return (carry[0] + fold(dyx), carry[1] + fold(dy), carry[2] + fold(dh))

        zero = jnp.zeros((8, D), F32)
        sums = lax.fori_loop(0, rows // step, body, (zero, zero, zero))
        for row, value in zip((GAIN + k, SHIFT + k, bias), sums):
            grad[row : row + 1, :] += jnp.sum(value, 0, keepdims=True)
        return exchange(f.at[pl.ds(0, rows)], f.at[pl.ds(rows, rows)])

    def hidden(s, i, x, gl, gp):
        def body(t):
            cols = pl.ds(al(i * wide + t * 256), 256)
            u = dot(x[...], R.wi[:, cols], NN) + vin[s : s + 1, pl.ds(al(g.c * hf + i * wide + t * 256), 256)]
            phi = 0.5 + 0.5 * lax.erf(u * (1.0 / math.sqrt(2.0)))
            gl[:, cols] = (u * phi).astype(BF16)
            gp[:, cols] = (phi + u * (jnp.exp(-0.5 * (u * u)) * (1.0 / math.sqrt(2.0 * math.pi)))).astype(BF16)

        tiles(wide // 256, body)

    def hidden_back(s, f, gl, gp, du, half):
        def body(i):
            t = half * (hf // 512) + i
            cols = pl.ds(al(t * 256), 256)
            value = dot(f[...], R.wf[cols, :], NT) * gp[:, cols].astype(F32)
            du[:, cols] = value.astype(BF16)
            per = D // 256
            row = VECTORS + s * (FF // D) + g.c * (hf // D) + t // per
            grad[pl.ds(row, 1), pl.ds(al(lax.rem(t, per) * 256), 256)] = jnp.sum(value, 0, keepdims=True)
            R.wf[cols, :] = dot(gl[:, cols], f[...], TN).astype(BF16)

        tiles(hf // 512, body)

    def hidden_weight(i, x, du):
        def body(t):
            cols = pl.ds(al(t * 128), 128)
            at = pl.ds(i * wide, wide)
            R.wi[cols, at] = dot(x[:, cols], du[:, at], TN).astype(BF16)

        tiles(D // 128, body)

    def context_back(f, wo, dc):
        def body(t):
            cols = pl.ds(al(t * 128), 128)
            dc[:, cols] = dot(f[...], wo[cols, :], NT).astype(BF16)

        tiles(h // 128, body)

    def out_weight(wo, fs, contexts):
        def body(t):
            cols = pl.ds(al(t * 128), 128)
            wo[cols, :] = sum(dot(c[:, cols], f[...], TN) for f, c in zip(fs, contexts)).astype(BF16)

        tiles(h // 128, body)

    def qkv_weight(wq, j, xs, dqs):
        def body(t):
            cols = pl.ds(al(t * 256), 256)
            wq[j, cols, :] = sum(dot(x[:, cols], dq[j], TN) for x, dq in zip(xs, dqs)).astype(BF16)

        tiles(D // 256, body)

    def qkv_back(acc, sb, rb, dq, wq):
        return halves(acc, sb, rb, lambda cols: sum(dot(dq[j], wq[j, cols, :], NT) for j in range(3)))

    def pump(i):
        line[i].forward_x()
        if i + AHEAD < len(line):
            line[i + AHEAD].start_x()
        if i == 0:
            q0.forward_y0()
        elif i == 1:
            q0.forward_y()
            o0.forward_y0()
        elif i == 2:
            o0.forward_y()

    done = {}

    def step(*tensors):
        for x in tensors:
            x.stage(done.get(x.t, 0))
            done[x.t] = done.get(x.t, 0) + 1

    for i in range(3):
        pump(i)
    q0.arrived()
    for s in S:
        project(0, R.x0[s], R.wq0, R.qkv0[s])
    pump(3)
    attend(0, 1, R.qkv0[0], R.qkv0[1], R.p0[0], R.c0[0], 2)
    pump(4)
    attend(1, 0, R.qkv0[1], R.qkv0[0], R.p0[1], R.c0[1], 2)
    o0.arrived()
    part = [
        halves(R.acc[s], R.sb[s], R.rb[s], lambda cols, s=s: dot(R.c0[s][...], R.wo0[:, cols], NN)) for s in S
    ]
    pump(5)
    x1_own, x1_core, x1_y, x1_far = [], [], [], []
    for s in S:
        k = n[s]
        part[s].wait()
        norm(
            lambda at, s=s: R.x0[s][at, :].astype(F32),
            R.acc[s], R.rb[s], R.xh0[s], R.rr0[s], 0, ATT_BIAS + 2, R.x1o[s],
        )
        x1_own.append(load(R.x1o[s], R.x1.at[pl.ds(0, k)], False))
        x1_core.append(exchange(R.x1o[s], R.x1.at[pl.ds(2 * k, k)], None, False))
        x1_y.append(exchange(R.x1o[s], R.x1.at[pl.ds(k, k)], g.y_peer, False))
        x1_far.append(exchange(R.x1.at[pl.ds(k, k)], R.x1.at[pl.ds(3 * k, k)], None, False))

        def keep(s=s):
            x1_own[s].start()
            x1_core[s].start()

        pl.when(this(s))(keep)
        pl.when(that(s))(x1_y[s].start)

    def private(s):
        m, k = 1 + s, n[s]
        k2, k4 = 2 * k, 4 * k
        top = lambda ref, rows: ref.at[pl.ds(0, rows)]
        third = lambda ref: ref.at[:, pl.ds(0, k4)]
        x1, x2 = top(R.x1, k4), top(R.x2, k4)
        qkv, dq, ctx, dc = third(R.qkv), third(R.dq), top(R.c, k4), top(R.dc, k4)
        acc, sb, rb, ds = (top(v, k2) for v in (R.accp, R.sbp, R.rbp, R.dsp))
        gl, gp, du = (top(v, k4) for v in (R.g, R.gp, R.du))
        xh, rr = [R.xh.at[i, pl.ds(0, k2)] for i in S], [R.rr.at[i, pl.ds(0, k2)] for i in S]
        f1, f2 = (R.f.at[i, pl.ds(0, k4)] for i in S)
        x1_y[s].wait_recv()
        x1_far[s].start()
        x1_own[s].wait()
        x1_core[s].wait_recv()
        x1_far[s].wait_recv()
        for x in qp:
            x.arrived()
        project(m, x1, R.wq, qkv)
        pump(6)
        attend(s, s, qkv, qkv, R.p, ctx, 4)
        op.arrived()
        out1 = halves(acc, sb, rb, lambda cols: dot(ctx[...], R.wo[:, cols], NN))
        pump(7)
        out1.wait()
        norm(lambda at: x1[at, :].astype(F32), acc, rb, xh[0], rr[0], 1 + s, ATT_BIAS + 3 * m + 2, top(x2, k2))
        x2_core = exchange(top(x2, k2), x2.at[pl.ds(k2, k2)])
        ip[0].arrived()
        x2_core.wait_recv()
        hidden(s, 0, x2, gl, gp)
        pump(8)
        ip[1].arrived()
        hidden(s, 1, x2, gl, gp)
        pump(9)
        for x in fp:
            x.arrived()
        out2 = halves(acc, sb, rb, lambda cols: dot(gl[...], R.wf[:, cols], NN))
        out2.wait()
        norm(
            lambda at: xh[0][at, :] * row_of(GAIN + 1 + s) + row_of(SHIFT + 1 + s),
            acc, rb, xh[1], rr[1], 3 + s, OUT_BIAS + s, top(R.yp, k2),
        )
        y_out[s].start()
        cot_own[s].wait()
        cot_other[s].wait_recv()
        row_at = lax.broadcasted_iota(jnp.int32, (k, 128 + n[1]), 0) + 128 * s
        same = row_at == lax.broadcasted_iota(jnp.int32, (k, 128 + n[1]), 1)
        for i in S:
            value = jnp.sum(jnp.where(same, R.keys[i, 0:1, :], 0.0), -1, keepdims=True)
            R.row_live[i * k : (i + 1) * k, :] = jnp.broadcast_to(value, (k, 128))

        def cot_of(at):
            return jnp.where(R.row_live[at, 0:1] == 0.0, R.cot[at, :].astype(F32), 0.0)

        f_core = norm_back(cot_of, ds, xh[1], rr[1], 3 + s, OUT_BIAS + s, f2)
        for x in line:
            x.drain()
        f_core.wait()
        for half in range(2):
            hidden_back(s, f2, gl, gp, du, half)
            fp[0].send_x(1, half)
        fp[1].send()
        din = halves(acc, sb, rb, lambda cols: dot(du[...], R.wi[cols, :], NT))
        for i, x in enumerate(ip):
            hidden_weight(i, x2, du)
            x.send()
        din.wait()
        back = lambda at: ds[at, :] + (acc[at, :] + rb[at, :].astype(F32))
        f_core = norm_back(back, ds, xh[0], rr[0], 1 + s, ATT_BIAS + 3 * m + 2, f1)
        step(fp[0])
        f_core.wait()
        context_back(f1, R.wo, dc)
        out_weight(R.wo, [f1], [ctx])
        op.send()
        attend_back(s, s, qkv, qkv, R.p, dc, dq, dq, m, 4)
        step(fp[1])
        dx = qkv_back(acc, sb, rb, dq, R.wq)
        for j in range(3):
            qkv_weight(R.wq, j, [x1], [dq])
            qp[j].send()
        step(fp[0], ip[0])
        dx.wait()

        def split(i):
            at = pl.ds(al(i * 16, 16), 16)
            low = pl.ds(al(k + i * 16, 16), 16)
            R.dy[s][at, :] = back(at)
            R.dgive[at, :] = back(low).astype(BF16)

        tiles(k // 16, split)
        dy_give[s].start()
        step(fp[0], fp[1])
        x1_core[s].wait_send()
        x1_far[s].wait_send()
        x2_core.wait_send()
        x1_y[1 - s].wait_send()
        cot_other[1 - s].wait_send()

    y_out = [exchange(R.yp.at[pl.ds(n[s], n[s])], R.yin.at[pl.ds(0, n[s])], g.y_peer, False) for s in S]
    dy_give = [exchange(R.dgive.at[pl.ds(0, n[s])], R.dtake.at[pl.ds(0, n[s])], g.y_peer, False) for s in S]
    pl.when(this(0))(functools.partial(private, 0))
    done.clear()
    pl.when(this(1))(functools.partial(private, 1))

    f0 = []
    for s in S:

        def take(s=s):
            dy_give[s].wait_recv()

            def body(i):
                at = pl.ds(al(i * 16, 16), 16)
                R.dy[s][at, :] = R.dtake[at, :].astype(F32)

            tiles(n[s] // 16, body)

        pl.when(that(s))(take)
        f0.append(
            norm_back(lambda at, s=s: R.dy[s][at, :], R.ds[s], R.xh0[s], R.rr0[s], 0, ATT_BIAS + 2, R.f0[s])
        )
    step(ip[1])
    for s in S:
        f0[s].wait()
        context_back(R.f0[s], R.wo0, R.dc0[s])
    out_weight(R.wo0, R.f0, R.c0)
    o0.send()
    step(ip[0], op)
    attend_back(0, 1, R.qkv0[0], R.qkv0[1], R.p0[0], R.dc0[0], R.dq0[0], R.dq0[1], 0, 2)
    step(fp[1], ip[1], o0)
    attend_back(1, 0, R.qkv0[1], R.qkv0[0], R.p0[1], R.dc0[1], R.dq0[1], R.dq0[0], 0, 2)

    def vector_round(i, device):
        return rcopy(grad, R.grad_in.at[i], sems.ws.at[i], sems.wr.at[i], device)

    def vector_far(i, half, device):
        return rcopy(R.grad_half.at[half], R.grad_far.at[i], sems.ws.at[2 + i], sems.wr.at[2 + i], device)

    first, second = vector_round(0, g.core_peer), vector_round(1, g.y_peer)
    inner = [vector_far(d - 1, 0, g.in_peer(d)) for d in range(1, g.B)]
    outer = [vector_far(g.B + d - 2, 1, g.out_peer(d)) for d in range(1, g.A)]
    first.start()
    part = [qkv_back(R.acc[s], R.sb[s], R.rb[s], R.dq0[s], R.wq0) for s in S]
    first.wait()
    grad[...] += R.grad_in[0]
    second.start()
    step(qp[0])
    qkv_weight(R.wq0, 2 - 2 * g.y, R.x0, R.dq0)
    q0.back_y().start()
    qkv_weight(R.wq0, 1, R.x0, R.dq0)
    q0.send_x(1)
    second.wait()
    grad[...] += R.grad_in[1]
    R.grad_half[0] = grad[...].astype(BF16)
    for x in inner:
        x.start()
    qkv_weight(R.wq0, 2 * g.y, R.x0, R.dq0)
    step(qp[1], op, qp[2], q0, qp[0], o0)
    for s in S:
        part[s].wait()

        def body(i, s=s):
            at = pl.ds(al(i * 16, 16), 16)
            R.dx[s][at, :] = R.ds[s][at, :] + (R.acc[s][at, :] + R.rb[s][at, :].astype(F32))

        tiles(n[s] // 16, body)
    puts = [pltpu.make_async_copy(R.dx[s], out.dx[s], sems.out.at[s]) for s in S]
    for put in puts:
        put.start()
    own_y = [pltpu.make_async_copy(R.yp.at[pl.ds(0, n[s])], out.y[s], sems.out.at[2]) for s in S]
    in_y = [pltpu.make_async_copy(R.yin.at[pl.ds(0, n[s])], out.y[s], sems.out.at[3]) for s in S]

    def put_y(s):
        own_y[s].start()
        y_out[1 - s].wait_recv()
        in_y[1 - s].start()

    for s in S:
        pl.when(this(s))(functools.partial(put_y, s))
    for x in inner:
        x.wait()
    for d in range(1, g.B):
        grad[...] += R.grad_far[d - 1].astype(F32)
    R.grad_half[1] = grad[...].astype(BF16)
    for x in outer:
        x.start()
    step(qp[1], q0, qp[2], o0, q0)
    for x in outer:
        x.wait()
    for d in range(1, g.A):
        grad[...] += R.grad_far[g.B + d - 2].astype(F32)
    final = pltpu.make_async_copy(grad, out.grad, sems.out.at[4])
    final.start()
    last = fp + ip + [op] + qp + [o0, q0]
    while any(done[x.t] < x.stages for x in last):
        for x in last:
            if done[x.t] < x.stages:
                step(x)
    for x in last:
        x.finish()
    for put in puts:
        put.wait()

    def end(s):
        own_y[s].wait()
        in_y[1 - s].wait()
        y_out[s].wait_send()
        dy_give[s].wait_send()

    for s in S:
        pl.when(this(s))(functools.partial(end, s))
    final.wait()
    for d in range(1, g.A):
        vec_z(d).wait_send()
    for d in range(1, g.B):
        for k in range(g.A):
            vec_x(d, k).wait_send()
    for copy in x0_other + key_other:
        copy.wait_send()


def local(
    words,
    regions,
    word_count,
    region_count,
    attn_qkv,
    attn_out,
    attn_bias,
    ffn_in,
    ffn_in_bias,
    ffn_out,
    ffn_out_bias,
    norm_gain,
    norm_bias,
    word_cot,
    region_cot,
    *,
    dp,
    F,
):
    items, nw, D = words.shape
    nr = regions.shape[1]
    FF = ffn_in.shape[2]
    h, hf = D // 2, FF // 2
    A, B = OUTER, F // OUTER
    n = (items * nw, items * nr)
    most = max(n)
    f = lax.axis_index("fsdp")

    small, wide = D // F, FF // F
    lanes = max(window(small, F), window(wide, F))
    at_row = lambda v, row: jnp.pad(v, ((row, VECTORS + 8 - row - v.shape[0]), (0, lanes - v.shape[1])))
    pieces = [attn_bias[0], attn_bias[1], attn_bias[2], ffn_out_bias, norm_gain, norm_bias, ffn_in_bias]
    vectors = sum(at_row(v, row) for v, row in zip(pieces, (0, 3, 6, 9, 11, 16, VECTORS)))

    inputs = dict(
        x=[words.reshape(n[0], D), regions.reshape(n[1], D)],
        live=[word_count, region_count],
        cot=[word_cot.reshape(n[0], D), region_cot.reshape(n[1], D)],
        vectors=vectors,
        attn_qkv=attn_qkv,
        attn_out=attn_out,
        ffn_in=ffn_in,
        ffn_out=ffn_out,
    )
    rs, rf = D // F, FF // F
    rows = VECTORS + 2 * (FF // D)
    shape = jax.ShapeDtypeStruct
    outputs = dict(
        y=[shape((k, D), BF16) for k in n],
        dx=[shape((k, D), F32) for k in n],
        q=shape((3, 3, rs, D), BF16),
        o=shape((3, rs, D), BF16),
        i=shape((2, rs, FF), BF16),
        f=shape((2, rf, D), BF16),
        grad=shape((rows, D), F32),
    )
    dma = pltpu.SemaphoreType.DMA
    slots = A * (B - 1)
    V = lambda *dims: pltpu.VMEM(dims, BF16)
    W = lambda *dims: pltpu.VMEM(dims, F32)

    def shared(total, r, w, *whole):
        return dict(
            y=V(total, w),
            x=[V(slots, r, w) for _ in S],
            z=[V(A - 1, r, w) for _ in S],
            y2=[V(r, w) for _ in S],
            c=V(*whole),
        )

    def private(r, w, half):
        used = slots - A // 2 if half else slots
        return dict(x=[V(1, 8, 128), V(used, r, w)], z=[V(1, 8, 128), V(A - 1, r, w)], fin=V(3, r, w))

    def both(make):
        return [make(k) for k in n]

    T = 10
    scratch = dict(
        wq0=V(3, D, h),
        wo0=V(h, D),
        wq=V(3, D, h),
        wo=V(h, D),
        wi=V(D, hf),
        wf=V(hf, D),
        gq0=shared(D, rs, h, 3, rs, h),
        go0=shared(h, rs, D // 3, rs, D),
        gq=[private(rs, h, False) for _ in range(3)],
        go=private(rs, D, True),
        gi=[private(rs, hf // 2, False) for _ in S],
        gf=[private(rf, D // 2, True) for _ in S],
        vec_in=V(F, VECTORS + 8, lanes),
        vec=W(VECTORS, D + 128),
        vin=W(8, FF + 128),
        grad=W(rows, D),
        grad_in=W(2, rows, D),
        grad_half=V(2, rows, D),
        grad_far=V(B - 1 + A - 1, rows, D),
        keys=W(4, 8, 128 + n[1]),
        masks=W(4, n[0] + n[1], 128 + n[1]),
        x0=both(lambda k: V(2 * k, D)),
        qkv0=both(lambda k: V(3, 2 * k, h)),
        dq0=both(lambda k: V(3, 2 * k, h)),
        c0=both(lambda k: V(2 * k, h)),
        dc0=both(lambda k: V(2 * k, h)),
        p0=[W(HEADS, n[s], n[1 - s]) for s in S],
        acc=both(lambda k: W(k, D)),
        sb=both(lambda k: V(k, D)),
        rb=both(lambda k: V(k, D)),
        xh0=both(lambda k: W(k, D)),
        rr0=both(lambda k: W(k, 128)),
        x1o=both(lambda k: V(k, D)),
        dy=both(lambda k: W(k, D)),
        ds=both(lambda k: W(k, D)),
        f0=both(lambda k: V(2 * k, D)),
        dx=both(lambda k: W(k, D)),
        x1=V(4 * most, D),
        x2=V(4 * most, D),
        qkv=V(3, 4 * most, h),
        dq=V(3, 4 * most, h),
        c=V(4 * most, h),
        dc=V(4 * most, h),
        p=W(2 * HEADS, most, most),
        accp=W(2 * most, D),
        sbp=V(2 * most, D),
        rbp=V(2 * most, D),
        dsp=W(2 * most, D),
        xh=W(2, 2 * most, D),
        rr=W(2, 2 * most, 128),
        f=V(2, 4 * most, D),
        g=V(4 * most, hf),
        gp=V(4 * most, hf),
        du=V(4 * most, hf),
        cot=V(2 * most, D),
        row_live=W(2 * most, 128),
        yp=V(2 * most, D),
        yin=V(most, D),
        dgive=V(most, D),
        dtake=V(most, D),
        sem=dict(
            own=dma((T, 2)),
            zs=dma((T, 2, A - 1)),
            zr=dma((T, 2, A - 1)),
            xs=dma((T, 2, slots)),
            xr=dma((T, 2, slots)),
            ys=dma((T, A)),
            yr=dma((T, A)),
            gys=dma((T,)),
            gyr=dma((T,)),
            gxs=dma((T, 2, slots)),
            gxr=dma((T, 2, slots)),
            gzs=dma((T, 2, A - 1)),
            gzr=dma((T, 2, A - 1)),
            gws=dma((T, 2)),
            gwr=dma((T, 2)),
            gcs=dma((T,)),
            gcr=dma((T,)),
            fs=dma((T, 3)),
            fr=dma((T, 3)),
            put=dma((T, 4)),
            es=dma((48,)),
            er=dma((48,)),
            load=dma((12,)),
            vzs=dma((A - 1,)),
            vzr=dma((A - 1,)),
            vxs=dma((slots,)),
            vxr=dma((slots,)),
            ws=dma((2 + A - 1 + B - 1,)),
            wr=dma((2 + A - 1 + B - 1,)),
            out=dma((5,)),
        ),
    )

    any_spec = pl.BlockSpec(memory_space=pl.ANY)
    leaf = lambda v: not isinstance(v, (dict, list, tuple))
    tree = jax.tree.structure((inputs, outputs, scratch), is_leaf=leaf)
    out_list, out_tree = jax.tree.flatten(outputs, is_leaf=leaf)
    in_list = jax.tree.leaves(inputs, is_leaf=leaf)
    made = pl.pallas_call(
        functools.partial(kernel, tree, (F, D, FF, n, items)),
        out_shape=out_list,
        in_specs=[pl.BlockSpec(memory_space=pltpu.SMEM) if v.ndim == 1 else any_spec for v in in_list],
        out_specs=[any_spec] * len(out_list),
        scratch_shapes=jax.tree.leaves(scratch, is_leaf=leaf),
        compiler_params=pltpu.CompilerParams(
            collective_id=0, has_side_effects=True, vmem_limit_bytes=67_000_000
        ),
        name="layer",
    )(*in_list)
    got = spaces(jax.tree.unflatten(out_tree, made))

    def over_groups(value):
        total = value
        for k in range(1, dp // 4):
            total = total + lax.ppermute(value, "dp", [(r, (r + 4 * k) % dp) for r in range(dp)])
        return total

    weights = [over_groups(v.astype(F32) if dp == 4 else v).astype(F32) for v in (got.q, got.o, got.i, got.f)]
    sums = over_groups(got.grad)
    near = lax.dynamic_slice(sums[:VECTORS], (0, f * small), (VECTORS, small))
    far = lax.dynamic_slice(sums[VECTORS:].reshape(2, FF), (0, f * wide), (2, wide))
    return (
        got.y[0].reshape(words.shape),
        got.y[1].reshape(regions.shape),
        got.dx[0].reshape(words.shape),
        got.dx[1].reshape(regions.shape),
        weights[0],
        weights[1],
        near[:9].reshape(3, 3, small),
        weights[2],
        far,
        weights[3],
        near[9:11],
        near[11:16],
        near[16:21],
    )


def solution(mesh):
    both = ("dp", "fsdp")
    rows = P(both, None, None)
    third, second = P(None, None, "fsdp", None), P(None, "fsdp", None)
    params = (third, second, P(None, None, "fsdp"), second, P(None, "fsdp"), second) + (P(None, "fsdp"),) * 3
    return jax.shard_map(
        functools.partial(local, dp=mesh.shape["dp"], F=mesh.shape["fsdp"]),
        mesh=mesh,
        in_specs=(rows, rows, P(both), P(both)) + params + (rows, rows),
        out_specs=(rows,) * 4 + params,
        check_vma=False,
    )
```

```python
import functools
import math
from types import SimpleNamespace

import jax
import jax.numpy as jnp
from jax import lax
from jax.experimental import pallas as pl
from jax.experimental.pallas import tpu as pltpu
from jax.sharding import PartitionSpec as P

HEADS = 12
HEAD_DIM = 64
EPS = 1e-06
NEG = -1e30
OUTER = 4
VECTORS = 24
AHEAD = 5
BF16 = jnp.bfloat16
F32 = jnp.float32
MESH = pl.DeviceIdType.MESH
S = (0, 1)
NN = ((1,), (0,))
NT = ((1,), (1,))
TN = ((0,), (0,))


def window(size, devices):
    worst = max((size * f) % 128 for f in range(devices))
    return -(-(size + worst) // 128) * 128


def al(value, step=128):
    return pl.multiple_of(value, step)


def rcopy(src, dst, send, recv, device):
    return pltpu.make_async_remote_copy(
        src_ref=src, dst_ref=dst, send_sem=send, recv_sem=recv, device_id=device, device_id_type=MESH
    )


def dot(a, b, dims):
    return lax.dot_general(a, b, (dims, ((), ())), preferred_element_type=F32)


def spaces(tree):
    if isinstance(tree, dict):
        return SimpleNamespace(**{k: spaces(v) for k, v in tree.items()})
    if isinstance(tree, list):
        return [spaces(v) for v in tree]
    return tree


def tiles(count, body):
    def run(t, carry):
        body(t)
        return carry

    lax.fori_loop(0, count, run, 0)


def add_rows(into, terms, rows, fresh=False):
    step = 32 if rows % 32 == 0 else 16 if rows % 16 == 0 else 8

    def body(i):
        at = pl.ds(al(i * step, step), step)
        value = None if fresh else into[at, :].astype(F32)
        for term in terms:
            more = term[at, :].astype(F32)
            value = more if value is None else value + more
        into[at, :] = value.astype(BF16)

    tiles(rows // step, body)


class Place:
    def __init__(self, fsdp):
        self.A, self.F = OUTER, fsdp
        self.B = fsdp // OUTER
        r, f = lax.axis_index("dp"), lax.axis_index("fsdp")
        self.r, self.f = r, f
        self.c, self.y = lax.rem(r, 2), lax.rem(r // 2, 2)
        self.o, self.b = f // self.B, lax.rem(f, self.B)
        self.core_peer = (r + 1 - 2 * self.c, f)
        self.y_peer = (r + 2 - 4 * self.y, f)
        self.far_peer = (r + 3 - 4 * self.y - 2 * self.c, f)

    def out_at(self, o):
        return (self.r, o * self.B + self.b)

    def out_peer(self, d):
        return self.out_at(lax.rem(self.o + d, self.A))

    def in_peer(self, d):
        return (self.r, self.o * self.B + lax.rem(self.b + d, self.B))

    def peers(self):
        return (
            [self.core_peer, self.y_peer, self.far_peer]
            + [self.out_peer(d) for d in range(1, self.A)]
            + [self.in_peer(d) for d in range(1, self.B)]
        )


class Ways:
    def __init__(self, outer, middle, step=128):
        self.outer, self.middle, self.step = outer, middle, step

    def own(self, y):
        at = y * (self.outer + self.middle)
        return (al(at, self.step) if self.step > 1 else at), self.outer

    def both(self):
        return self.outer, self.middle

    def other(self, y):
        return self.own(1 - y)


class Tensor:
    def __init__(self, g, t, src, view, rows, half, ways, sems, bufs, out, whole=None):
        self.g, self.t, self.src, self.view, self.whole = g, t, src, view, whole
        self.rs, self.split, self.ways, self.sems, self.bufs, self.out = rows, half, ways, sems, bufs, out
        self.private = whole is None
        self.qs = (1,) if self.private else (0, 1)
        self.stages = 3 if self.private else 6

    def sem(self, array, *at):
        return array.at[(self.t, *at)]

    def keys(self):
        g = self.g
        if self.split:
            return [(k, g.c * (g.A // 2) + k) for k in range(g.A // 2)]
        return [(d, lax.rem(g.o + g.A - d, g.A)) for d in (0, 2, 3, 1)[: g.A]]

    def row(self, o, b):
        g = self.g
        at = (o * g.B + b) * self.rs
        if self.split:
            at = lax.rem(at, (g.F // 2) * self.rs)
        return al(at, 8)

    def inset(self):
        return self.g.o // (self.g.A // 2) == self.g.c

    def mine(self, fn):
        if self.split:
            pl.when(self.inset())(fn)
        else:
            fn()

    def others(self, fn):
        if self.split:
            pl.when(jnp.logical_not(self.inset()))(fn)
        else:
            fn()

    def cols(self, q, back=False):
        way = self.ways
        return way.own(self.g.y) if q == 0 else way.both()

    def part(self, q, o, b, back=False):
        return self.view(self.row(o, b), self.rs, *self.cols(q, back))


    def own_copy(self, q):
        g = self.g
        return pltpu.make_async_copy(
            self.src(*self.cols(q)), self.part(q, g.o, g.b), self.sem(self.sems.own, q)
        )

    def zcopy(self, q, d):
        g = self.g
        slot = lax.rem(g.o, g.A // 2) if self.split else d - 1
        return rcopy(
            self.src(*self.cols(q)),
            self.part(q, g.o, g.b),
            self.sem(self.sems.zs, q, d - 1),
            self.sem(self.sems.zr, q, slot),
            g.out_peer(d),
        )

    def xcopy(self, q, d, k, o, from_src=False):
        g = self.g
        v = self.part(q, o, g.b)
        i = (d - 1) * g.A + k
        return rcopy(
            self.src(*self.cols(q)) if from_src else v,
            v,
            self.sem(self.sems.xs, q, i),
            self.sem(self.sems.xr, q, i),
            g.in_peer(d),
        )

    def ycopy(self, k, o):
        g = self.g
        v = self.view(self.row(o, 0), self.rs * g.B, *self.cols(0))
        return rcopy(v, v, self.sem(self.sems.ys, k), self.sem(self.sems.yr, k), g.y_peer)

    def own_slot(self):
        return lax.rem(self.g.o, self.g.A // 2) if self.split else 0

    def start_z(self):
        def go():
            for q in self.qs:
                for d in (2, 3, 1)[: self.g.A - 1]:
                    self.zcopy(q, d).start()

        self.mine(go)

    def start_x(self):
        g = self.g

        def go():
            for q in self.qs:
                self.own_copy(q).start()
                for d in range(1, g.B):
                    self.xcopy(q, d, self.own_slot(), g.o, True).start()

        self.mine(go)

    def forward_x(self):
        g = self.g
        for q in self.qs:
            for k, o in self.keys():

                def go(k=k, o=o, q=q):
                    v = self.part(q, o, g.b)
                    slot = k if self.split else k - 1
                    rcopy(
                        v, v, self.sem(self.sems.zs, q, 0), self.sem(self.sems.zr, q, slot), g.out_peer(1)
                    ).wait_recv()
                    for d in range(1, g.B):
                        self.xcopy(q, d, k, o).start()

                if self.split:
                    pl.when(o != g.o)(go)
                elif k > 0:
                    go()

    def x_arrived(self, q, k, o):
        g = self.g
        for d in range(1, g.B):
            v = self.part(q, o, lax.rem(g.b + g.B - d, g.B))
            i = (d - 1) * g.A + k
            rcopy(v, v, self.sem(self.sems.xs, q, i), self.sem(self.sems.xr, q, i), g.in_peer(1)).wait_recv()

    def forward_y0(self):
        g = self.g

        def go():
            k = self.own_slot()
            self.own_copy(0).wait()
            self.x_arrived(0, k, g.o)
            self.ycopy(k, g.o).start()

        self.mine(go)

    def forward_y(self):
        g = self.g
        for k, o in self.keys():

            def go(k=k, o=o):
                self.x_arrived(0, k, o)
                self.ycopy(k, o).start()

            if self.split:
                pl.when(o != g.o)(go)
            elif k > 0:
                go()

    def arrived(self):
        g = self.g
        self.mine(lambda: self.own_copy(1).wait())
        for k, o in self.keys():
            self.x_arrived(1, k, o)
            if not self.private:
                v = self.view(self.row(o, 0), self.rs * g.B, *self.ways.other(g.y))
                rcopy(v, v, self.sem(self.sems.ys, k), self.sem(self.sems.yr, k), g.y_peer).wait_recv()

    def drain(self):
        g = self.g

        def go():
            for q in self.qs:
                for d in range(1, g.A):
                    self.zcopy(q, d).wait_send()

        self.mine(go)
        for k, o in self.keys():
            for q in self.qs:
                for d in range(1, g.B):
                    self.xcopy(q, d, k, o).wait_send()
            if not self.private:
                self.ycopy(k, o).wait_send()


    def total_rows(self):
        return self.rs * (self.g.F // 2 if self.split else self.g.F)

    def owners(self):
        g = self.g
        if self.split:
            return [(k, g.c * (g.A // 2) + k) for k in range(g.A // 2)]
        return [(d, lax.rem(g.o + d, g.A)) for d in (2, 3, 1, 0)]

    def back_y(self):
        g = self.g
        v = self.view(0, self.total_rows(), *self.ways.other(g.y))
        return rcopy(v, self.bufs.y, self.sem(self.sems.gys), self.sem(self.sems.gyr), g.y_peer)

    def back_x(self, q, d, k, o, b):
        g = self.g
        i = (d - 1) * g.A + k
        return rcopy(
            self.part(q, o, b, True),
            self.bufs.x[q].at[i],
            self.sem(self.sems.gxs, q, i),
            self.sem(self.sems.gxr, q, i),
            g.in_peer(d),
        )

    def back_z(self, q, k, o):
        g = self.g
        slot = lax.rem(o - g.o + g.A, g.A) - 1 if self.split else k - 1
        return rcopy(
            self.part(q, o, g.b, True),
            self.bufs.z[q].at[slot],
            self.sem(self.sems.gzs, q, k if self.split else k - 1),
            self.sem(self.sems.gzr, q, slot),
            g.out_at(o),
        )

    def each_z(self, q, k, o, way):
        if self.split:
            pl.when(o != self.g.o)(lambda: way(self.back_z(q, k, o)))
        elif k > 0:
            way(self.back_z(q, k, o))

    def back_y2(self, q):
        g = self.g
        return rcopy(
            self.part(q, g.o, g.b, True),
            self.bufs.y2[q],
            self.sem(self.sems.gws, q),
            self.sem(self.sems.gwr, q),
            g.y_peer,
        )

    def back_core(self):
        g = self.g
        return rcopy(
            self.whole(self.row(g.o, g.b), self.rs),
            self.bufs.c,
            self.sem(self.sems.gcs),
            self.sem(self.sems.gcr),
            g.core_peer,
        )

    def put_own(self):
        g = self.g
        return pltpu.make_async_copy(
            self.whole(self.row(g.o, g.b), self.rs), self.out(g.c), self.sem(self.sems.put, 0)
        )

    def put_other(self):
        return pltpu.make_async_copy(self.bufs.c, self.out(1 - self.g.c), self.sem(self.sems.put, 1))

    def fin(self, i):
        g = self.g
        return rcopy(
            self.part(1, g.o, g.b),
            self.bufs.fin.at[i],
            self.sem(self.sems.fs, i),
            self.sem(self.sems.fr, i),
            (g.core_peer, g.y_peer, g.far_peer)[i],
        )

    def put(self, i):
        g = self.g
        c = (1 - g.c, g.c, 1 - g.c, g.c)[i]
        y = (g.y, 1 - g.y, 1 - g.y, g.y)[i]
        source = self.part(1, g.o, g.b) if i == 3 else self.bufs.fin.at[i]
        return pltpu.make_async_copy(source, self.out(y, c), self.sem(self.sems.put, i))

    def taken(self):
        return ((1,), (0, 2)) if self.split else ((0, 1, 2), ())

    def send(self):
        if not self.private:
            self.back_y().start()
        self.send_x(1)

    def send_x(self, q, only=None):
        g = self.g
        for k, o in self.owners():
            if only is None or k == only:
                for d in range(1, g.B):
                    self.back_x(q, d, k, o, lax.rem(g.b + d, g.B)).start()

    def take_y(self):
        self.back_y().wait_recv()
        rows = self.total_rows()
        add_rows(self.view(0, rows, *self.cols(0, True)), [self.bufs.y], rows)
        self.send_x(0)

    def take_x(self, q):
        g = self.g
        for k, o in self.owners():
            terms = []
            for d in range(1, g.B):
                self.back_x(q, d, k, o, g.b).wait_recv()
                terms.append(self.bufs.x[q].at[(d - 1) * g.A + k])
            if terms:
                add_rows(self.part(q, o, g.b, True), terms, self.rs)
            self.each_z(q, k, o, lambda copy: copy.start())

    def take_z(self, q):
        g = self.g

        def go():
            v = self.part(q, g.o, g.b, True)
            for d in range(g.A - 1):
                rcopy(
                    v,
                    self.bufs.z[q].at[d],
                    self.sem(self.sems.gzs, q, 0),
                    self.sem(self.sems.gzr, q, d),
                    g.out_peer(1),
                ).wait_recv()
            add_rows(v, [self.bufs.z[q].at[d] for d in range(g.A - 1)], self.rs)
            if self.private:
                for i in range(3):
                    self.fin(i).start()
                self.put(3).start()
            else:
                self.back_y2(q).start()

        self.mine(go)

    def take_y2(self, q):
        g = self.g

        def go():
            self.back_y2(q).wait()
            if q == 1:
                add_rows(self.part(1, g.o, g.b, True), [self.bufs.y2[1]], self.rs)
            else:
                self.back_y().wait_send()
                at = self.view(self.row(g.o, g.b), self.rs, *self.ways.other(g.y))
                add_rows(at, [self.bufs.y2[0]], self.rs, fresh=True)
                self.back_core().start()
                self.put_own().start()

        self.mine(go)
        if q == 0 and self.split:
            self.others(lambda: self.back_y().wait_send())

    def take_core(self):
        def go():
            self.back_core().wait_recv()
            self.put_other().start()

        self.others(go)

    def take_fin(self):
        def go(which):
            for i in which:
                self.fin(i).wait_recv()
                self.put(i).start()

        self.mine(lambda: go(self.taken()[0]))
        self.others(lambda: go(self.taken()[1]))

    def stage(self, n):
        if self.private:
            if n == 0:
                self.take_x(1)
            elif n == 1:
                self.take_z(1)
            elif n == 2:
                self.take_fin()
        elif n == 0:
            self.take_y()
        elif n == 1:
            self.take_x(1)
        elif n == 2:
            self.take_x(0)
            self.take_z(1)
        elif n == 3:
            self.take_z(0)
            self.take_y2(1)
        elif n == 4:
            self.take_y2(0)
        elif n == 5:
            self.take_core()

    def finish(self):
        g = self.g
        for q in self.qs:
            for d in range(1, g.B):
                for k, o in self.owners():
                    self.back_x(q, d, k, o, g.b).wait_send()
            for k, o in self.owners():
                self.each_z(q, k, o, lambda copy: copy.wait_send())

        def mine():
            if self.private:
                for i in range(3):
                    self.fin(i).wait_send()
                for i in self.taken()[0] + (3,):
                    self.put(i).wait()
            else:
                self.back_core().wait_send()
                self.put_own().wait()

        def others():
            if self.private:
                for i in self.taken()[1]:
                    self.put(i).wait()
            else:
                self.put_other().wait()

        self.mine(mine)
        self.others(others)


def kernel(tree, sizes, *refs):
    inp, out, R = (spaces(part) for part in jax.tree.unflatten(tree, refs))
    F, D, FF, n, items = sizes
    g = Place(F)
    h, hf = D // 2, FF // 2
    scale = HEAD_DIM ** (-0.5)
    pairs = HEADS // 4
    sems = R.sem

    meet = pltpu.get_barrier_semaphore()
    peers = g.peers()
    for peer in peers:
        pl.semaphore_signal(meet, inc=1, device_id=peer, device_id_type=MESH)
    pl.semaphore_wait(meet, len(peers))

    rs, rf = D // F, FF // F
    line = []

    def make(*args):
        line.append(Tensor(g, len(line), *args))
        return line[-1]

    q0 = make(
        lambda j, k: inp.attn_qkv.at[0, j, :, pl.ds(al(g.c * h), h)],
        lambda r, k, j, kj: R.wq0.at[j, pl.ds(r, k), :],
        rs,
        False,
        Ways(1, 1, 1),
        sems,
        R.gq0,
        lambda c: out.q.at[0, :, :, pl.ds(al(c * h), h)],
        lambda r, k: R.wq0.at[:, pl.ds(r, k), :],
    )
    o0 = make(
        lambda j, k: inp.attn_out.at[0, :, pl.ds(j, k)],
        lambda r, k, j, kj: R.wo0.at[pl.ds(r, k), pl.ds(j, kj)],
        rs,
        True,
        Ways(D // 3, D // 3),
        sems,
        R.go0,
        lambda c: out.o.at[0],
        lambda r, k: R.wo0.at[pl.ds(r, k), :],
    )
    qp = [
        make(
            lambda j, k, i=i: inp.attn_qkv.at[1 + g.y, i, :, pl.ds(al(g.c * h), h)],
            lambda r, k, j, kj, i=i: R.wq.at[i, pl.ds(r, k), :],
            rs,
            False,
            Ways(0, h),
            sems,
            R.gq[i],
            lambda y, c, i=i: out.q.at[1 + y, i, :, pl.ds(al(c * h), h)],
        )
        for i in range(3)
    ]
    op = make(
        lambda j, k: inp.attn_out.at[1 + g.y],
        lambda r, k, j, kj: R.wo.at[pl.ds(r, k), :],
        rs,
        True,
        Ways(0, D),
        sems,
        R.go,
        lambda y, c: out.o.at[1 + y],
    )
    wide, long = hf // 2, D // 2
    ip = [
        make(
            lambda j, k, i=i: inp.ffn_in.at[g.y, :, pl.ds(al(g.c * hf + i * wide), wide)],
            lambda r, k, j, kj, i=i: R.wi.at[pl.ds(r, k), pl.ds(i * wide, wide)],
            rs,
            False,
            Ways(0, wide),
            sems,
            R.gi[i],
            lambda y, c, i=i: out.i.at[y, :, pl.ds(al(c * hf + i * wide), wide)],
        )
        for i in range(2)
    ]
    fp = [
        make(
            lambda j, k, i=i: inp.ffn_out.at[g.y, :, pl.ds(i * long, long)],
            lambda r, k, j, kj, i=i: R.wf.at[pl.ds(r, k), pl.ds(i * long, long)],
            rf,
            True,
            Ways(0, long),
            sems,
            R.gf[i],
            lambda y, c, i=i: out.f.at[y, :, pl.ds(i * long, long)],
        )
        for i in range(2)
    ]

    slot_of = lambda f: R.vec_in.at[f]

    def vec_z(d):
        return rcopy(inp.vectors, slot_of(g.f), sems.vzs.at[d - 1], sems.vzr.at[d - 1], g.out_peer(d))

    def vec_x(d, k):
        o = lax.rem(g.o + g.A - k, g.A)
        at = slot_of(o * g.B + g.b)
        i = (d - 1) * g.A + k
        return rcopy(inp.vectors if k == 0 else at, at, sems.vxs.at[i], sems.vxr.at[i], g.in_peer(d))

    for d in range(1, g.A):
        vec_z(d).start()
    for d in range(1, g.B):
        vec_x(d, 0).start()

    count = [0, 0]

    def exchange(src, dst, device=None, start=True):
        i = count[0]
        count[0] += 1
        copy = rcopy(src, dst, sems.es.at[i], sems.er.at[i], g.core_peer if device is None else device)
        if start:
            copy.start()
        return copy

    def load(src, dst, start=True):
        i = count[1]
        count[1] += 1
        copy = pltpu.make_async_copy(src, dst, sems.load.at[i])
        if start:
            copy.start()
        return copy

    def this(s):
        return g.y == s

    def that(s):
        return g.y != s

    x0_own = [load(inp.x[s], R.x0[s].at[pl.ds(0, n[s])]) for s in S]
    x0_other = [exchange(inp.x[s], R.x0[s].at[pl.ds(n[s], n[s])]) for s in S]

    def item_of(at, slots):
        return sum((at >= slots * i).astype(jnp.int32) for i in range(1, items))

    lane = lax.broadcasted_iota(jnp.int32, (8, 128 + n[1]), 1)
    slots = [n[s] // items for s in S]
    alive = jnp.zeros((8, 128 + n[1]), jnp.int32)
    for s in S:
        for i in range(items):
            start = 128 * s + slots[s] * i
            alive = alive + ((lane >= start) & (lane < start + inp.live[s][i])).astype(jnp.int32)
    R.keys[0] = jnp.where(alive > 0, 0.0, NEG)
    key_other = [
        exchange(R.keys.at[0], R.keys.at[i], device)
        for i, device in ((2, g.core_peer), (1, g.y_peer), (3, g.far_peer))
    ]
    vec_own = load(inp.vectors, slot_of(g.f))
    q0.start_z()
    q0.start_x()
    o0.start_z()
    o0.start_x()
    line[2].start_z()
    line[2].start_x()
    for x in line[3:]:
        x.start_z()
    for x in line[3:AHEAD]:
        x.start_x()
    cot_own = [load(inp.cot[s], R.cot.at[pl.ds(0, n[s])], False) for s in S]
    cot_other = [exchange(inp.cot[s], R.cot.at[pl.ds(n[s], n[s])], g.y_peer, False) for s in S]
    for s in S:
        pl.when(this(s))(cot_own[s].start)
        pl.when(that(s))(cot_other[s].start)

    for k in range(1, g.A):
        o = lax.rem(g.o + g.A - k, g.A)
        at = slot_of(o * g.B + g.b)
        rcopy(at, at, sems.vzs.at[0], sems.vzr.at[k - 1], g.out_peer(1)).wait_recv()
        for d in range(1, g.B):
            vec_x(d, k).start()
    for d in range(1, g.B):
        for k in range(g.A):
            o = lax.rem(g.o + g.A - k, g.A)
            at = slot_of(o * g.B + lax.rem(g.b + g.B - d, g.B))
            i = (d - 1) * g.A + k
            rcopy(at, at, sems.vxs.at[i], sems.vxr.at[i], g.in_peer(1)).wait_recv()
    vec_own.wait()
    vec, vin, grad = R.vec, R.vin, R.grad
    vec[...] = jnp.zeros_like(vec)
    vin[...] = jnp.zeros_like(vin)
    grad[...] = jnp.zeros_like(grad)
    for f in range(F):
        for into, low, high, size in ((vec, 0, VECTORS, D // F), (vin, VECTORS, VECTORS + 8, FF // F)):
            start, turn, span = size * f // 128 * 128, size * f % 128, window(size, F)
            piece = R.vec_in[f, low:high, 0:span].astype(F32)
            into[:, start : start + span] += pltpu.roll(piece, turn, 1) if turn else piece

    def row_of(i):
        return vec[i : i + 1, 0:D]

    ATT_BIAS, OUT_BIAS, GAIN, SHIFT = 0, 9, 11, 16

    for copy in key_other:
        copy.wait_recv()

    def build(b):
        lane = lax.broadcasted_iota(jnp.int32, (1, 128 + n[1]), 1)
        key_item = jnp.where(lane < 128, item_of(lane, n[0] // items), item_of(lane - 128, n[1] // items))
        for s in S:
            query_item = item_of(lax.broadcasted_iota(jnp.int32, (n[s], 1), 0), n[s] // items)
            rows = pl.ds(s * n[0], n[s])
            R.masks[b, rows, :] = jnp.where(query_item == key_item, R.keys[b, 0:1, :], NEG)

    tiles(4, build)
    for s in S:
        x0_own[s].wait()
    for s in S:
        x0_other[s].wait_recv()

    def project(m, x, wq, qkv):
        for j in range(3):
            value = dot(x[...], wq[j], NN)
            if j != 1:
                row = ATT_BIAS + 3 * m + (0 if j == 0 else 1)
                value = value + vec[row : row + 1, pl.ds(al(g.c * h), h)]
            qkv[j] = value.astype(BF16)

    def mask_of(b, qs, ks):
        return R.masks[b, pl.ds(qs * n[0], n[qs]), pl.ds(ks * 128, n[ks])]

    def attend(qs, ks, q_ref, kv_ref, probs, context, total):
        def body(b):
            qr, kr = pl.ds(al(b * n[qs], 16), n[qs]), pl.ds(al(b * n[ks], 16), n[ks])
            mask = mask_of(b * (4 // total), qs, ks)
            cut = lambda ref, j, rows, i: ref[j, rows, i * HEAD_DIM : (i + 1) * HEAD_DIM]
            heads = range(2 * pairs)
            scores = [dot(cut(q_ref, 0, qr, i), cut(kv_ref, 1, kr, i), NT) * scale + mask for i in heads]
            tops = [jnp.max(v, -1, keepdims=True) for v in scores]
            exs = [jnp.exp(v - top) for v, top in zip(scores, tops)]
            sums = [1.0 / jnp.sum(v, -1, keepdims=True) for v in exs]
            shares = [v * k for v, k in zip(exs, sums)]
            parts = [dot(pr.astype(BF16), cut(kv_ref, 2, kr, i), NN) for i, pr in enumerate(shares)]
            made = [jnp.concatenate(parts[2 * p : 2 * p + 2], 1).astype(BF16) for p in range(pairs)]
            for i, pr in enumerate(shares):
                probs[2 * pairs * b + i, 0 : n[qs], 0 : n[ks]] = pr
            for p, value in enumerate(made):
                context[qr, p * 128 : (p + 1) * 128] = value

        tiles(total, body)

    def attend_back(qs, ks, q_ref, kv_ref, probs, dc_ref, dq_ref, dkv_ref, m, total):
        def body(b):
            qr, kr = pl.ds(al(b * n[qs], 16), n[qs]), pl.ds(al(b * n[ks], 16), n[ks])
            cut = lambda ref, j, rows, i: ref[j, rows, i * HEAD_DIM : (i + 1) * HEAD_DIM]
            heads = range(2 * pairs)
            dcs = [dc_ref[qr, i * HEAD_DIM : (i + 1) * HEAD_DIM] for i in heads]
            prs = [probs[2 * pairs * b + i, 0 : n[qs], 0 : n[ks]] for i in heads]
            dps = [dot(d, cut(kv_ref, 2, kr, i), NT) for i, d in enumerate(dcs)]
            dvs = [dot(pr.astype(BF16), d, TN) for pr, d in zip(prs, dcs)]
            sums = [jnp.sum(pr * dp, -1, keepdims=True) for pr, dp in zip(prs, dps)]
            dss = [(pr * (dp - k)).astype(BF16) for pr, dp, k in zip(prs, dps, sums)]
            dqs = [dot(ds, cut(kv_ref, 1, kr, i), NN) * scale for i, ds in enumerate(dss)]
            dks = [dot(ds, cut(q_ref, 0, qr, i), TN) * scale for i, ds in enumerate(dss)]
            made = [[jnp.concatenate(v[2 * p : 2 * p + 2], 1) for v in (dqs, dks, dvs)] for p in range(pairs)]
            row = ATT_BIAS + 3 * m
            for p, (dq, dk, dv) in enumerate(made):
                cols = slice(p * 128, (p + 1) * 128)
                dq_ref[0, qr, cols] = dq.astype(BF16)
                dkv_ref[1, kr, cols] = dk.astype(BF16)
                dkv_ref[2, kr, cols] = dv.astype(BF16)
            for p, (dq, dk, dv) in enumerate(made):
                lanes = pl.ds(al(g.c * h + p * 128), 128)
                grad[row : row + 1, lanes] += jnp.sum(dq, 0, keepdims=True)
                grad[row + 1 : row + 2, lanes] += jnp.sum(dv, 0, keepdims=True)

        tiles(total, body)

    def halves(acc, sb, rb, product, step=256):
        rows = acc.shape[0]

        def body(t):
            cols = pl.ds(al(t * step), step)
            value = product(cols)
            acc[:, cols] = value[:rows]
            sb[:, cols] = value[rows:].astype(BF16)

        tiles(D // step, body)
        return exchange(sb, rb)

    def block(rows):
        return next(k for k in (48, 80, 32, 16) if rows % k == 0)

    def norm(base, acc, rb, xh, rr, k, bias, into):
        step = block(acc.shape[0])

        def body(i):
            at = pl.ds(al(i * step, 16), step)
            total = base(at) + ((acc[at, :] + rb[at, :].astype(F32)) + row_of(bias))
            centered = total - jnp.mean(total, -1, keepdims=True)
            spread = lax.rsqrt(jnp.mean(centered * centered, -1, keepdims=True) + EPS)
            xhat = centered * spread
            xh[at, :] = xhat
            rr[at, :] = jnp.broadcast_to(spread, (step, 128))
            into[at, :] = (xhat * row_of(GAIN + k) + row_of(SHIFT + k)).astype(BF16)

        tiles(acc.shape[0] // step, body)

    def norm_back(dy_of, ds, xh, rr, k, bias, f):
        rows = ds.shape[0]
        step = block(rows)

        def body(i, carry):
            at = pl.ds(al(i * step, 16), step)
            dy = dy_of(at)
            xhat = xh[at, :]
            dx = dy * row_of(GAIN + k)
            dyx = dy * xhat
            mean_dx = jnp.mean(dx, -1, keepdims=True)
            mean_dxx = jnp.mean(dx * xhat, -1, keepdims=True)
            dh = rr[at, 0:1] * (dx - mean_dx - xhat * mean_dxx)
            ds[at, :] = dh
            f[at, :] = dh.astype(BF16)
            fold = lambda v: sum(v[j : j + 8] for j in range(0, step, 8))
            return (carry[0] + fold(dyx), carry[1] + fold(dy), carry[2] + fold(dh))

        zero = jnp.zeros((8, D), F32)
        sums = lax.fori_loop(0, rows // step, body, (zero, zero, zero))
        for row, value in zip((GAIN + k, SHIFT + k, bias), sums):
            grad[row : row + 1, :] += jnp.sum(value, 0, keepdims=True)
        return exchange(f.at[pl.ds(0, rows)], f.at[pl.ds(rows, rows)])

    def hidden(s, i, x, gl, gp):
        def body(t):
            cols = pl.ds(al(i * wide + t * 256), 256)
            u = dot(x[...], R.wi[:, cols], NN) + vin[s : s + 1, pl.ds(al(g.c * hf + i * wide + t * 256), 256)]
            phi = 0.5 + 0.5 * lax.erf(u * (1.0 / math.sqrt(2.0)))
            gl[:, cols] = (u * phi).astype(BF16)
            gp[:, cols] = (phi + u * (jnp.exp(-0.5 * (u * u)) * (1.0 / math.sqrt(2.0 * math.pi)))).astype(BF16)

        tiles(wide // 256, body)

    def hidden_back(s, f, gl, gp, du, half):
        def body(i):
            t = half * (hf // 512) + i
            cols = pl.ds(al(t * 256), 256)
            value = dot(f[...], R.wf[cols, :], NT) * gp[:, cols].astype(F32)
            du[:, cols] = value.astype(BF16)
            per = D // 256
            row = VECTORS + s * (FF // D) + g.c * (hf // D) + t // per
            grad[pl.ds(row, 1), pl.ds(al(lax.rem(t, per) * 256), 256)] = jnp.sum(value, 0, keepdims=True)
            R.wf[cols, :] = dot(gl[:, cols], f[...], TN).astype(BF16)

        tiles(hf // 512, body)

    def hidden_weight(i, x, du):
        def body(t):
            cols = pl.ds(al(t * 128), 128)
            at = pl.ds(i * wide, wide)
            R.wi[cols, at] = dot(x[:, cols], du[:, at], TN).astype(BF16)

        tiles(D // 128, body)

    def context_back(f, wo, dc):
        def body(t):
            cols = pl.ds(al(t * 128), 128)
            dc[:, cols] = dot(f[...], wo[cols, :], NT).astype(BF16)

        tiles(h // 128, body)

    def out_weight(wo, fs, contexts):
        def body(t):
            cols = pl.ds(al(t * 128), 128)
            wo[cols, :] = sum(dot(c[:, cols], f[...], TN) for f, c in zip(fs, contexts)).astype(BF16)

        tiles(h // 128, body)

    def qkv_weight(wq, j, xs, dqs):
        def body(t):
            cols = pl.ds(al(t * 256), 256)
            wq[j, cols, :] = sum(dot(x[:, cols], dq[j], TN) for x, dq in zip(xs, dqs)).astype(BF16)

        tiles(D // 256, body)

    def qkv_back(acc, sb, rb, dq, wq):
        return halves(acc, sb, rb, lambda cols: sum(dot(dq[j], wq[j, cols, :], NT) for j in range(3)))

    def pump(i):
        line[i].forward_x()
        if i + AHEAD < len(line):
            line[i + AHEAD].start_x()
        if i == 0:
            q0.forward_y0()
        elif i == 1:
            q0.forward_y()
            o0.forward_y0()
        elif i == 2:
            o0.forward_y()

    done = {}

    def step(*tensors):
        for x in tensors:
            x.stage(done.get(x.t, 0))
            done[x.t] = done.get(x.t, 0) + 1

    for i in range(3):
        pump(i)
    q0.arrived()
    for s in S:
        project(0, R.x0[s], R.wq0, R.qkv0[s])
    pump(3)
    attend(0, 1, R.qkv0[0], R.qkv0[1], R.p0[0], R.c0[0], 2)
    pump(4)
    attend(1, 0, R.qkv0[1], R.qkv0[0], R.p0[1], R.c0[1], 2)
    o0.arrived()
    part = [
        halves(R.acc[s], R.sb[s], R.rb[s], lambda cols, s=s: dot(R.c0[s][...], R.wo0[:, cols], NN)) for s in S
    ]
    pump(5)
    x1_own, x1_core, x1_y, x1_far = [], [], [], []
    for s in S:
        k = n[s]
        part[s].wait()
        norm(
            lambda at, s=s: R.x0[s][at, :].astype(F32),
            R.acc[s], R.rb[s], R.xh0[s], R.rr0[s], 0, ATT_BIAS + 2, R.x1o[s],
        )
        x1_own.append(load(R.x1o[s], R.x1.at[pl.ds(0, k)], False))
        x1_core.append(exchange(R.x1o[s], R.x1.at[pl.ds(2 * k, k)], None, False))
        x1_y.append(exchange(R.x1o[s], R.x1.at[pl.ds(k, k)], g.y_peer, False))
        x1_far.append(exchange(R.x1.at[pl.ds(k, k)], R.x1.at[pl.ds(3 * k, k)], None, False))

        def keep(s=s):
            x1_own[s].start()
            x1_core[s].start()

        pl.when(this(s))(keep)
        pl.when(that(s))(x1_y[s].start)

    def private(s):
        m, k = 1 + s, n[s]
        k2, k4 = 2 * k, 4 * k
        top = lambda ref, rows: ref.at[pl.ds(0, rows)]
        third = lambda ref: ref.at[:, pl.ds(0, k4)]
        x1, x2 = top(R.x1, k4), top(R.x2, k4)
        qkv, dq, ctx, dc = third(R.qkv), third(R.dq), top(R.c, k4), top(R.dc, k4)
        acc, sb, rb, ds = (top(v, k2) for v in (R.accp, R.sbp, R.rbp, R.dsp))
        gl, gp, du = (top(v, k4) for v in (R.g, R.gp, R.du))
        xh, rr = [R.xh.at[i, pl.ds(0, k2)] for i in S], [R.rr.at[i, pl.ds(0, k2)] for i in S]
        f1, f2 = (R.f.at[i, pl.ds(0, k4)] for i in S)
        x1_y[s].wait_recv()
        x1_far[s].start()
        x1_own[s].wait()
        x1_core[s].wait_recv()
        x1_far[s].wait_recv()
        for x in qp:
            x.arrived()
        project(m, x1, R.wq, qkv)
        pump(6)
        attend(s, s, qkv, qkv, R.p, ctx, 4)
        op.arrived()
        out1 = halves(acc, sb, rb, lambda cols: dot(ctx[...], R.wo[:, cols], NN))
        pump(7)
        out1.wait()
        norm(lambda at: x1[at, :].astype(F32), acc, rb, xh[0], rr[0], 1 + s, ATT_BIAS + 3 * m + 2, top(x2, k2))
        x2_core = exchange(top(x2, k2), x2.at[pl.ds(k2, k2)])
        ip[0].arrived()
        x2_core.wait_recv()
        hidden(s, 0, x2, gl, gp)
        pump(8)
        ip[1].arrived()
        hidden(s, 1, x2, gl, gp)
        pump(9)
        for x in fp:
            x.arrived()
        out2 = halves(acc, sb, rb, lambda cols: dot(gl[...], R.wf[:, cols], NN))
        out2.wait()
        norm(
            lambda at: xh[0][at, :] * row_of(GAIN + 1 + s) + row_of(SHIFT + 1 + s),
            acc, rb, xh[1], rr[1], 3 + s, OUT_BIAS + s, top(R.yp, k2),
        )
        y_out[s].start()
        cot_own[s].wait()
        cot_other[s].wait_recv()
        row_at = lax.broadcasted_iota(jnp.int32, (k, 128 + n[1]), 0) + 128 * s
        same = row_at == lax.broadcasted_iota(jnp.int32, (k, 128 + n[1]), 1)
        for i in S:
            value = jnp.sum(jnp.where(same, R.keys[i, 0:1, :], 0.0), -1, keepdims=True)
            R.row_live[i * k : (i + 1) * k, :] = jnp.broadcast_to(value, (k, 128))

        def cot_of(at):
            return jnp.where(R.row_live[at, 0:1] == 0.0, R.cot[at, :].astype(F32), 0.0)

        f_core = norm_back(cot_of, ds, xh[1], rr[1], 3 + s, OUT_BIAS + s, f2)
        for x in line:
            x.drain()
        f_core.wait()
        for half in range(2):
            hidden_back(s, f2, gl, gp, du, half)
            fp[0].send_x(1, half)
        fp[1].send()
        din = halves(acc, sb, rb, lambda cols: dot(du[...], R.wi[cols, :], NT))
        for i, x in enumerate(ip):
            hidden_weight(i, x2, du)
            x.send()
        din.wait()
        back = lambda at: ds[at, :] + (acc[at, :] + rb[at, :].astype(F32))
        f_core = norm_back(back, ds, xh[0], rr[0], 1 + s, ATT_BIAS + 3 * m + 2, f1)
        step(fp[0])
        f_core.wait()
        context_back(f1, R.wo, dc)
        out_weight(R.wo, [f1], [ctx])
        op.send()
        attend_back(s, s, qkv, qkv, R.p, dc, dq, dq, m, 4)
        step(fp[1])
        dx = qkv_back(acc, sb, rb, dq, R.wq)
        for j in range(3):
            qkv_weight(R.wq, j, [x1], [dq])
            qp[j].send()
        step(fp[0], ip[0])
        dx.wait()

        def split(i):
            at = pl.ds(al(i * 16, 16), 16)
            low = pl.ds(al(k + i * 16, 16), 16)
            R.dy[s][at, :] = back(at)
            R.dgive[at, :] = back(low).astype(BF16)

        tiles(k // 16, split)
        dy_give[s].start()
        step(fp[0], fp[1])
        x1_core[s].wait_send()
        x1_far[s].wait_send()
        x2_core.wait_send()
        x1_y[1 - s].wait_send()
        cot_other[1 - s].wait_send()

    y_out = [exchange(R.yp.at[pl.ds(n[s], n[s])], R.yin.at[pl.ds(0, n[s])], g.y_peer, False) for s in S]
    dy_give = [exchange(R.dgive.at[pl.ds(0, n[s])], R.dtake.at[pl.ds(0, n[s])], g.y_peer, False) for s in S]
    pl.when(this(0))(functools.partial(private, 0))
    done.clear()
    pl.when(this(1))(functools.partial(private, 1))

    f0 = []
    for s in S:

        def take(s=s):
            dy_give[s].wait_recv()

            def body(i):
                at = pl.ds(al(i * 16, 16), 16)
                R.dy[s][at, :] = R.dtake[at, :].astype(F32)

            tiles(n[s] // 16, body)

        pl.when(that(s))(take)
        f0.append(
            norm_back(lambda at, s=s: R.dy[s][at, :], R.ds[s], R.xh0[s], R.rr0[s], 0, ATT_BIAS + 2, R.f0[s])
        )
    step(ip[1])
    for s in S:
        f0[s].wait()
        context_back(R.f0[s], R.wo0, R.dc0[s])
    out_weight(R.wo0, R.f0, R.c0)
    o0.send()
    step(ip[0], op)
    attend_back(0, 1, R.qkv0[0], R.qkv0[1], R.p0[0], R.dc0[0], R.dq0[0], R.dq0[1], 0, 2)
    step(fp[1], ip[1], o0)
    attend_back(1, 0, R.qkv0[1], R.qkv0[0], R.p0[1], R.dc0[1], R.dq0[1], R.dq0[0], 0, 2)

    def vector_round(i, device):
        return rcopy(grad, R.grad_in.at[i], sems.ws.at[i], sems.wr.at[i], device)

    def vector_far(i, half, device):
        return rcopy(R.grad_half.at[half], R.grad_far.at[i], sems.ws.at[2 + i], sems.wr.at[2 + i], device)

    first, second = vector_round(0, g.core_peer), vector_round(1, g.y_peer)
    inner = [vector_far(d - 1, 0, g.in_peer(d)) for d in range(1, g.B)]
    outer = [vector_far(g.B + d - 2, 1, g.out_peer(d)) for d in range(1, g.A)]
    first.start()
    part = [qkv_back(R.acc[s], R.sb[s], R.rb[s], R.dq0[s], R.wq0) for s in S]
    first.wait()
    grad[...] += R.grad_in[0]
    second.start()
    step(qp[0])
    qkv_weight(R.wq0, 2 - 2 * g.y, R.x0, R.dq0)
    q0.back_y().start()
    qkv_weight(R.wq0, 1, R.x0, R.dq0)
    q0.send_x(1)
    second.wait()
    grad[...] += R.grad_in[1]
    R.grad_half[0] = grad[...].astype(BF16)
    for x in inner:
        x.start()
    qkv_weight(R.wq0, 2 * g.y, R.x0, R.dq0)
    step(qp[1], op, qp[2], q0, qp[0], o0)
    for s in S:
        part[s].wait()

        def body(i, s=s):
            at = pl.ds(al(i * 16, 16), 16)
            R.dx[s][at, :] = R.ds[s][at, :] + (R.acc[s][at, :] + R.rb[s][at, :].astype(F32))

        tiles(n[s] // 16, body)
    puts = [pltpu.make_async_copy(R.dx[s], out.dx[s], sems.out.at[s]) for s in S]
    for put in puts:
        put.start()
    own_y = [pltpu.make_async_copy(R.yp.at[pl.ds(0, n[s])], out.y[s], sems.out.at[2]) for s in S]
    in_y = [pltpu.make_async_copy(R.yin.at[pl.ds(0, n[s])], out.y[s], sems.out.at[3]) for s in S]

    def put_y(s):
        own_y[s].start()
        y_out[1 - s].wait_recv()
        in_y[1 - s].start()

    for s in S:
        pl.when(this(s))(functools.partial(put_y, s))
    for x in inner:
        x.wait()
    for d in range(1, g.B):
        grad[...] += R.grad_far[d - 1].astype(F32)
    R.grad_half[1] = grad[...].astype(BF16)
    for x in outer:
        x.start()
    step(qp[1], q0, qp[2], o0, q0)
    for x in outer:
        x.wait()
    for d in range(1, g.A):
        grad[...] += R.grad_far[g.B + d - 2].astype(F32)
    final = pltpu.make_async_copy(grad, out.grad, sems.out.at[4])
    final.start()
    last = fp + ip + [op] + qp + [o0, q0]
    while any(done[x.t] < x.stages for x in last):
        for x in last:
            if done[x.t] < x.stages:
                step(x)
    for x in last:
        x.finish()
    for put in puts:
        put.wait()

    def end(s):
        own_y[s].wait()
        in_y[1 - s].wait()
        y_out[s].wait_send()
        dy_give[s].wait_send()

    for s in S:
        pl.when(this(s))(functools.partial(end, s))
    final.wait()
    for d in range(1, g.A):
        vec_z(d).wait_send()
    for d in range(1, g.B):
        for k in range(g.A):
            vec_x(d, k).wait_send()
    for copy in x0_other + key_other:
        copy.wait_send()


def local(
    words,
    regions,
    word_count,
    region_count,
    attn_qkv,
    attn_out,
    attn_bias,
    ffn_in,
    ffn_in_bias,
    ffn_out,
    ffn_out_bias,
    norm_gain,
    norm_bias,
    word_cot,
    region_cot,
    *,
    dp,
    F,
):
    items, nw, D = words.shape
    nr = regions.shape[1]
    FF = ffn_in.shape[2]
    h, hf = D // 2, FF // 2
    A, B = OUTER, F // OUTER
    n = (items * nw, items * nr)
    most = max(n)
    f = lax.axis_index("fsdp")

    small, wide = D // F, FF // F
    lanes = max(window(small, F), window(wide, F))
    at_row = lambda v, row: jnp.pad(v, ((row, VECTORS + 8 - row - v.shape[0]), (0, lanes - v.shape[1])))
    pieces = [attn_bias[0], attn_bias[1], attn_bias[2], ffn_out_bias, norm_gain, norm_bias, ffn_in_bias]
    vectors = sum(at_row(v, row) for v, row in zip(pieces, (0, 3, 6, 9, 11, 16, VECTORS)))

    inputs = dict(
        x=[words.reshape(n[0], D), regions.reshape(n[1], D)],
        live=[word_count, region_count],
        cot=[word_cot.reshape(n[0], D), region_cot.reshape(n[1], D)],
        vectors=vectors,
        attn_qkv=attn_qkv,
        attn_out=attn_out,
        ffn_in=ffn_in,
        ffn_out=ffn_out,
    )
    rs, rf = D // F, FF // F
    rows = VECTORS + 2 * (FF // D)
    shape = jax.ShapeDtypeStruct
    outputs = dict(
        y=[shape((k, D), BF16) for k in n],
        dx=[shape((k, D), F32) for k in n],
        q=shape((3, 3, rs, D), BF16),
        o=shape((3, rs, D), BF16),
        i=shape((2, rs, FF), BF16),
        f=shape((2, rf, D), BF16),
        grad=shape((rows, D), F32),
    )
    dma = pltpu.SemaphoreType.DMA
    slots = A * (B - 1)
    V = lambda *dims: pltpu.VMEM(dims, BF16)
    W = lambda *dims: pltpu.VMEM(dims, F32)

    def shared(total, r, w, *whole):
        return dict(
            y=V(total, w),
            x=[V(slots, r, w) for _ in S],
            z=[V(A - 1, r, w) for _ in S],
            y2=[V(r, w) for _ in S],
            c=V(*whole),
        )

    def private(r, w, half):
        used = slots - A // 2 if half else slots
        return dict(x=[V(1, 8, 128), V(used, r, w)], z=[V(1, 8, 128), V(A - 1, r, w)], fin=V(3, r, w))

    def both(make):
        return [make(k) for k in n]

    T = 10
    scratch = dict(
        wq0=V(3, D, h),
        wo0=V(h, D),
        wq=V(3, D, h),
        wo=V(h, D),
        wi=V(D, hf),
        wf=V(hf, D),
        gq0=shared(D, rs, h, 3, rs, h),
        go0=shared(h, rs, D // 3, rs, D),
        gq=[private(rs, h, False) for _ in range(3)],
        go=private(rs, D, True),
        gi=[private(rs, hf // 2, False) for _ in S],
        gf=[private(rf, D // 2, True) for _ in S],
        vec_in=V(F, VECTORS + 8, lanes),
        vec=W(VECTORS, D + 128),
        vin=W(8, FF + 128),
        grad=W(rows, D),
        grad_in=W(2, rows, D),
        grad_half=V(2, rows, D),
        grad_far=V(B - 1 + A - 1, rows, D),
        keys=W(4, 8, 128 + n[1]),
        masks=W(4, n[0] + n[1], 128 + n[1]),
        x0=both(lambda k: V(2 * k, D)),
        qkv0=both(lambda k: V(3, 2 * k, h)),
        dq0=both(lambda k: V(3, 2 * k, h)),
        c0=both(lambda k: V(2 * k, h)),
        dc0=both(lambda k: V(2 * k, h)),
        p0=[W(HEADS, n[s], n[1 - s]) for s in S],
        acc=both(lambda k: W(k, D)),
        sb=both(lambda k: V(k, D)),
        rb=both(lambda k: V(k, D)),
        xh0=both(lambda k: W(k, D)),
        rr0=both(lambda k: W(k, 128)),
        x1o=both(lambda k: V(k, D)),
        dy=both(lambda k: W(k, D)),
        ds=both(lambda k: W(k, D)),
        f0=both(lambda k: V(2 * k, D)),
        dx=both(lambda k: W(k, D)),
        x1=V(4 * most, D),
        x2=V(4 * most, D),
        qkv=V(3, 4 * most, h),
        dq=V(3, 4 * most, h),
        c=V(4 * most, h),
        dc=V(4 * most, h),
        p=W(2 * HEADS, most, most),
        accp=W(2 * most, D),
        sbp=V(2 * most, D),
        rbp=V(2 * most, D),
        dsp=W(2 * most, D),
        xh=W(2, 2 * most, D),
        rr=W(2, 2 * most, 128),
        f=V(2, 4 * most, D),
        g=V(4 * most, hf),
        gp=V(4 * most, hf),
        du=V(4 * most, hf),
        cot=V(2 * most, D),
        row_live=W(2 * most, 128),
        yp=V(2 * most, D),
        yin=V(most, D),
        dgive=V(most, D),
        dtake=V(most, D),
        sem=dict(
            own=dma((T, 2)),
            zs=dma((T, 2, A - 1)),
            zr=dma((T, 2, A - 1)),
            xs=dma((T, 2, slots)),
            xr=dma((T, 2, slots)),
            ys=dma((T, A)),
            yr=dma((T, A)),
            gys=dma((T,)),
            gyr=dma((T,)),
            gxs=dma((T, 2, slots)),
            gxr=dma((T, 2, slots)),
            gzs=dma((T, 2, A - 1)),
            gzr=dma((T, 2, A - 1)),
            gws=dma((T, 2)),
            gwr=dma((T, 2)),
            gcs=dma((T,)),
            gcr=dma((T,)),
            fs=dma((T, 3)),
            fr=dma((T, 3)),
            put=dma((T, 4)),
            es=dma((48,)),
            er=dma((48,)),
            load=dma((12,)),
            vzs=dma((A - 1,)),
            vzr=dma((A - 1,)),
            vxs=dma((slots,)),
            vxr=dma((slots,)),
            ws=dma((2 + A - 1 + B - 1,)),
            wr=dma((2 + A - 1 + B - 1,)),
            out=dma((5,)),
        ),
    )

    any_spec = pl.BlockSpec(memory_space=pl.ANY)
    leaf = lambda v: not isinstance(v, (dict, list, tuple))
    tree = jax.tree.structure((inputs, outputs, scratch), is_leaf=leaf)
    out_list, out_tree = jax.tree.flatten(outputs, is_leaf=leaf)
    in_list = jax.tree.leaves(inputs, is_leaf=leaf)
    made = pl.pallas_call(
        functools.partial(kernel, tree, (F, D, FF, n, items)),
        out_shape=out_list,
        in_specs=[pl.BlockSpec(memory_space=pltpu.SMEM) if v.ndim == 1 else any_spec for v in in_list],
        out_specs=[any_spec] * len(out_list),
        scratch_shapes=jax.tree.leaves(scratch, is_leaf=leaf),
        compiler_params=pltpu.CompilerParams(
            collective_id=0, has_side_effects=True, vmem_limit_bytes=67_000_000
        ),
        name="layer",
    )(*in_list)
    got = spaces(jax.tree.unflatten(out_tree, made))

    def over_groups(value):
        total = value
        for k in range(1, dp // 4):
            total = total + lax.ppermute(value, "dp", [(r, (r + 4 * k) % dp) for r in range(dp)])
        return total

    weights = [over_groups(v.astype(F32) if dp == 4 else v).astype(F32) for v in (got.q, got.o, got.i, got.f)]
    sums = over_groups(got.grad)
    near = lax.dynamic_slice(sums[:VECTORS], (0, f * small), (VECTORS, small))
    far = lax.dynamic_slice(sums[VECTORS:].reshape(2, FF), (0, f * wide), (2, wide))
    return (
        got.y[0].reshape(words.shape),
        got.y[1].reshape(regions.shape),
        got.dx[0].reshape(words.shape),
        got.dx[1].reshape(regions.shape),
        weights[0],
        weights[1],
        near[:9].reshape(3, 3, small),
        weights[2],
        far,
        weights[3],
        near[9:11],
        near[11:16],
        near[16:21],
    )


def solution(mesh):
    both = ("dp", "fsdp")
    rows = P(both, None, None)
    third, second = P(None, None, "fsdp", None), P(None, "fsdp", None)
    params = (third, second, P(None, None, "fsdp"), second, P(None, "fsdp"), second) + (P(None, "fsdp"),) * 3
    return jax.shard_map(
        functools.partial(local, dp=mesh.shape["dp"], F=mesh.shape["fsdp"]),
        mesh=mesh,
        in_specs=(rows, rows, P(both), P(both)) + params + (rows, rows),
        out_specs=(rows,) * 4 + params,
        check_vma=False,
    )
```
